32 devices in a mesh: gx: 4 (over y, x), gy: 8 (over z, core).
Axes of the slice: x: 2, y: 2, z: 4, core: 2. Of those that a mesh axis runs over, the one named last changes fastest.
Arguments:
- probes: float32 [24, 48, 64, 128], P('gx', 'gy'), may hold values from -6 to 6
- pair_blocks: float32 [24, 48, 9, 128, 128], P('gx', 'gy'), may hold values from -0.09375 to 0.09375
- partners: int32 [24, 48, 9], P('gx', 'gy'), may hold values from 0 to 1151, as said below
- shifts: int32 [2, 24, 48, 9], P(None, 'gx', 'gy'), may hold values from -1 to 1, as said below
- counts: int32 [24, 48], P('gx', 'gy'), may hold values from 1 to 9, as said below
- kpoint: float32 [2], replicated, may hold values from -3.140625 to 3.140625
Outputs:
- last_vector: float32 [24, 48, 64, 128], P('gx', 'gy')
- intersections: float32 [3, 2, 32], replicated
The draws below stay inside these ranges and needn't reach their ends.
Inputs may be any that keep to these rules, and one draw needn't show every extreme that they name: `partners`: slot 0 of cell (x, y) names the cell itself; slots 1 to 8 name its eight neighbouring cells (x + dx, y + dy) with dx, dy in -1..1 taken periodically modulo 24 and 48, each once, in no fixed order. shifts[0, x, y, s] = (x + dx - px) / 24 and shifts[1, x, y, s] = (y + dy - py) / 48 for the slot's offset (dx, dy) and partner cell (px, py). `counts`: slots at or beyond a cell's count are padding; some cell has all 9 slots live.
All inputs are finite; a program needn't handle non-finite values.
Results may differ from the reference program's by a relative error of at most 0.0001.
Values sent between devices are 32-bit elements; how exact they have to be, the bound alone decides.
A program may use at most 128 MiB of HBM per device.

```python
import math
import jax
import jax.numpy as jnp
from jax import lax

CX = 6
CY = 6
BLOCK = 128
SLOTS = 9
PROBES = 32
STEPS = 3
NCX = 24
NCY = 48
ROWS = 147456


def pair_layout(key):
    base = jax.random.fold_in(key, 7)
    first_key, second_key, third_key = jax.random.split(base, 3)
    bricks_x = NCX // CX
    bricks_y = NCY // CY
    dense_brick = jax.random.randint(first_key, (bricks_x, bricks_y), 0, 2)
    dense_brick = dense_brick.at[0, 0].set(1)
    cell_x = jnp.arange(NCX, dtype=jnp.int32)[:, None]
    cell_y = jnp.arange(NCY, dtype=jnp.int32)[None, :]
    dense = dense_brick[cell_x // CX, cell_y // CY]
    live = jax.random.randint(second_key, (NCX, NCY, 8), 0, 2)
    live = jnp.maximum(live, dense[:, :, None])
    scores = jax.random.randint(third_key, (NCX, NCY, 8), 0, 1 << 20) * 8 + jnp.arange(8, dtype=jnp.int32)
    ranking = (1 - live) * (1 << 24) + scores
    order = jnp.argsort(ranking, axis=-1, stable=True).astype(jnp.int32)
    table_x = jnp.array([-1, -1, -1, 0, 0, 1, 1, 1], jnp.int32)
    table_y = jnp.array([-1, 0, 1, -1, 1, -1, 0, 1], jnp.int32)
    offset_x = jnp.take(table_x, order)
    offset_y = jnp.take(table_y, order)
    zero = jnp.zeros((NCX, NCY, 1), jnp.int32)
    offset_x = jnp.concatenate([zero, offset_x], axis=-1)
    offset_y = jnp.concatenate([zero, offset_y], axis=-1)
    target_x = cell_x[:, :, None] + offset_x
    target_y = cell_y[:, :, None] + offset_y
    partner_x = jnp.mod(target_x, NCX)
    partner_y = jnp.mod(target_y, NCY)
    shift_x = jnp.floor_divide(target_x, NCX)
    shift_y = jnp.floor_divide(target_y, NCY)
    partners = (partner_x * NCY + partner_y).astype(jnp.int32)
    shifts = jnp.stack([shift_x, shift_y]).astype(jnp.int32)
    counts = (1 + jnp.sum(live, axis=-1)).astype(jnp.int32)
    return (partners, shifts, counts)


def draw_partners(key, part):
    return pair_layout(key)[0]


def draw_shifts(key, part):
    return pair_layout(key)[1]


def draw_counts(key, part):
    return pair_layout(key)[2]


def block_levels(stream_key, extent, cuts, least, high):
    factor_of, own = 1.0, jax.random.fold_in(stream_key, 6)
    for position, parts in cuts:
        steps = jnp.exp(jax.random.uniform(jax.random.fold_in(own, position), (parts,), jnp.float32, least / len(cuts), high / len(cuts)))
        factor_of = factor_of * jnp.repeat(steps, extent[position] // parts).reshape([-1 if axis == position else 1 for axis in range(len(extent))])
    return factor_of


def gaussian(own_key, shape, spread, bound, shards=(), kind=jnp.bfloat16):
    gain = block_levels(own_key, shape, shards, -0.22, 0.18) if shards else 1.0
    drawn = jax.random.normal(own_key, shape, jnp.float32) * spread * gain
    return jnp.minimum(jnp.maximum(drawn, -bound), bound).astype(kind)


def setup_inputs(seed: int = 0) -> dict:
    arg_keys = jax.random.split(jax.random.key(seed), 7)
    probes = gaussian(arg_keys[0], (NCX, NCY, 2 * PROBES, BLOCK), 1.0, 6.0, ((0, 4), (1, 8)), jnp.float32)
    pair_blocks = gaussian(arg_keys[1], (NCX, NCY, SLOTS, BLOCK, BLOCK), (4 * BLOCK * SLOTS) ** -0.5, 0.09375, ((0, 4), (1, 8)), jnp.float32)
    partners = draw_partners(jax.random.fold_in(arg_keys[6], 71), 0)
    shifts = draw_shifts(jax.random.fold_in(arg_keys[6], 71), 0)
    counts = draw_counts(jax.random.fold_in(arg_keys[6], 71), 0)
    kpoint = jnp.clip(jax.random.uniform(arg_keys[5], (2,), jnp.float32, -3.140625, 3.140625), -3.140625, 3.140625)
    return dict(probes=probes, pair_blocks=pair_blocks, partners=partners, shifts=shifts, counts=counts, kpoint=kpoint)


def apply_hamiltonian(field, blocks, flat_partner, cosine, sine):
    cells = flat_partner.shape[0]
    width = field.shape[2]
    half = width // 2
    source = field.reshape(cells, width, BLOCK)

    def accumulate(slot, sums):
        real_sum, imag_sum = sums
        piece = jnp.take(source, flat_partner[:, slot], axis=0)
        block = lax.dynamic_index_in_dim(blocks, slot, 1, keepdims=False)
        product = jnp.einsum('npb,nba->npa', piece, block, precision=lax.Precision.HIGHEST)
        cos_part = lax.dynamic_index_in_dim(cosine, slot, 1, keepdims=False)[:, None, None]
        sin_part = lax.dynamic_index_in_dim(sine, slot, 1, keepdims=False)[:, None, None]
        real_part = product[:, :half]
        imag_part = product[:, half:]
        return (real_sum + cos_part * real_part - sin_part * imag_part, imag_sum + sin_part * real_part + cos_part * imag_part)
    zeros = jnp.zeros((cells, half, BLOCK), jnp.float32)
    real_sum, imag_sum = lax.fori_loop(0, SLOTS, accumulate, (zeros, zeros))
    return jnp.concatenate([real_sum, imag_sum], axis=1).reshape(field.shape)

def intersection(first, other):
    half = first.shape[2] // 2
    first_re, first_im = (first[:, :, :half], first[:, :, half:])
    other_re, other_im = (other[:, :, :half], other[:, :, half:])
    real_part = lax.optimization_barrier(jnp.sum(first_re * other_re + first_im * other_im, axis=(0, 1, 3)))
    imag_part = lax.optimization_barrier(jnp.sum(first_re * other_im - first_im * other_re, axis=(0, 1, 3)))
    return jnp.stack([real_part, imag_part])

def reference(probes, pair_blocks, partners, shifts, counts, kpoint):
    cells = NCX * NCY
    flat_partner = partners.reshape(cells, SLOTS).astype(jnp.int32)
    angle = kpoint[0] * shifts[0].astype(jnp.float32) + kpoint[1] * shifts[1].astype(jnp.float32)
    angle = angle.reshape(cells, SLOTS)
    live = (jnp.arange(SLOTS, dtype=jnp.int32)[None, :] < counts.reshape(cells, 1)).astype(jnp.float32)
    cosine = jnp.cos(angle) * live
    sine = jnp.sin(angle) * live
    blocks = pair_blocks.reshape(cells, SLOTS, BLOCK, BLOCK)
    scale = 1.0 / math.sqrt(ROWS)
    before = probes
    current = apply_hamiltonian(probes, blocks, flat_partner, cosine, sine)
    found = [intersection(probes, current) * scale]
    for step in range(STEPS - 1):
        following = 2.0 * apply_hamiltonian(current, blocks, flat_partner, cosine, sine) - before
        before, current = (current, following)
        found.append(intersection(probes, current) * scale)
    return (current, jnp.stack(found))
```

```python
import functools
import math

import jax
import jax.numpy as jnp
from jax import lax
from jax.experimental import pallas as pl
from jax.experimental.pallas import tpu as pltpu
from jax.sharding import PartitionSpec as P

STEPS = 3
MESH = pl.DeviceIdType.MESH
F32, BF16 = jnp.float32, jnp.bfloat16


def kernel(
    axes, partners, counts, kpoint, v0_hbm, blocks_hbm, last, total,
    v0, v1, v2, halo_x, halo_y, field_a, field_b, landed, upper, lower, sums, ring_x, ring_y, table, turns,
    v0_sem, land_sem, send_sem, recv_sem, sum_send_x, sum_recv_x, sum_send_y, sum_recv_y,
):
    (name_x, size_x), (name_y, size_y) = axes
    cx, cy, width, block = v0.shape
    slots = landed.shape[1]
    half = width // 2
    pitch = cy + 2
    nothing = (cx + 2) * pitch
    me_x, me_y = lax.axis_index(name_x), lax.axis_index(name_y)
    total_x, total_y = cx * size_x, cy * size_y
    vectors = (v0, v1, v2, last)
    fields = (field_a, field_b)

    def landing(x, y):
        i = x * cy + y
        return pltpu.make_async_copy(blocks_hbm.at[x, y], landed.at[i], land_sem.at[i])

    inner = (cx - 2) * (cy - 2)

    def interior(k):
        return 1 + k // (cy - 2), 1 + k % (cy - 2)

    def rim_y(k):
        return 1 + k // 2, (k % 2) * (cy - 1)

    def mirror(step, y):
        return cy - 1 - y if step % 2 else y

    def rim_x(step, ys):
        return lambda k: ((k % 2) * (cx - 1), mirror(step, ys[k // 2]))

    wire = (0, cy - 1, cy - 2) + tuple(range(1, cy - 2))
    ready = ((cy - 1,), (0,)) + tuple((p - 1,) for p in range(2, cy - 3))
    ready = ready + ((cy - 4, cy - 3, cy - 2),)
    early = inner // 2

    for signal_name, size, me in ((name_x, size_x, me_x), (name_y, size_y, me_y)):
        for j in range(1, size):
            pl.semaphore_signal(
                pltpu.get_barrier_semaphore(),
                inc=1,
                device_id={signal_name: lax.rem(me + j, size)},
                device_id_type=MESH,
            )
    load_v0 = pltpu.make_async_copy(v0_hbm, v0, v0_sem)
    load_v0.start()
    for place, count in (
        (interior, inner),
        (rim_y, 2 * (cx - 2)),
        *((rim_x(0, ys), 2 * len(ys)) for ys in ready),
    ):
        if count > 6:

            @pl.loop(0, count)
            def _(k):
                landing(*place(k)).start()
        else:
            for k in range(count):
                landing(*place(k)).start()
    pl.semaphore_wait(pltpu.get_barrier_semaphore(), size_x + size_y - 2)

    def towards(name, size, me, side):
        return {name: lax.rem(me + (size - 1 if side else 1), size)}

    def remote(step, kind, src, dst, peer):
        return pltpu.make_async_remote_copy(
            src_ref=src,
            dst_ref=dst,
            send_sem=send_sem.at[step, kind],
            recv_sem=recv_sem.at[step, kind],
            device_id=peer,
            device_id_type=MESH,
        )

    def source(step):
        return vectors[step] if step else v0_hbm

    def x_copies(step, y):
        return [
            remote(
                step,
                2 * y + side,
                source(step).at[0 if side else cx - 1, y],
                halo_x.at[step, side, y],
                towards(name_x, size_x, me_x, side),
            )
            for side in range(2)
        ]

    def y_copy(step, side, x, length):
        return remote(
            step,
            2 * cy + 3 * side + (0 if x == 0 else 1 if x == 1 else 2),
            source(step).at[pl.ds(x, length), 0 if side else cy - 1],
            halo_y.at[step, side, pl.ds(1 + x, length)],
            towards(name_y, size_y, me_y, side),
        )

    def y_middles(step):
        return [y_copy(step, side, 1, cx - 2) for side in range(2)]

    def y_ends(step, side):
        return [y_copy(step, side, x, 1) for x in (0, cx - 1)]

    def corner_copies(step, side):
        return [
            remote(
                step,
                2 * cy + 6 + 2 * side + end,
                halo_x.at[step, end, 0 if side else cy - 1],
                halo_y.at[step, side, end * (cx + 1)],
                towards(name_y, size_y, me_y, side),
            )
            for end in range(2)
        ]

    def start(copies):
        for copy in copies:
            copy.start()

    def arrive(copies):
        for copy in copies:
            copy.wait_recv()

    def put(field, position, value):
        high = value.astype(BF16)
        field[position, :width] = high
        field[position, width:] = (value - high.astype(F32)).astype(BF16)

    def put_turned(field, position, value, at_x, at_y):
        entry = at_x * 3 + at_y
        cosine, sine = turns[0, entry : entry + 1], turns[1, entry : entry + 1]
        real, imag = value[:half], value[half:]
        put(
            field,
            position,
            jnp.concatenate(
                [cosine * real - sine * imag, sine * real + cosine * imag], axis=0
            ),
        )

    def put_x(step, y):
        for side in range(2):
            put_turned(
                fields[step % 2],
                side * (cx + 1) * pitch + y + 1,
                halo_x[step, side, y],
                2 * side,
                1,
            )

    def put_y(step, side, x, at_x):
        put_turned(
            fields[step % 2],
            x * pitch + side * (cy + 1),
            halo_y[step, side, x],
            at_x,
            2 * side,
        )

    def prepare(x, y):
        i = x * cy + y
        count = counts[x, y]
        for s in range(slots):
            partner = partners[x, y, s]
            partner_x = (partner * (((1 << 20) + total_y - 1) // total_y)) >> 20
            at_x = partner_x - me_x * cx + 1
            at_x = jnp.where(at_x < 0, at_x + total_x, at_x)
            at_x = jnp.where(at_x >= total_x, at_x - total_x, at_x)
            at_y = partner - partner_x * total_y - me_y * cy + 1
            at_y = jnp.where(at_y < 0, at_y + total_y, at_y)
            at_y = jnp.where(at_y >= total_y, at_y - total_y, at_y)
            at = jnp.minimum(jnp.maximum(at_x * pitch + at_y, 0), nothing - 1)
            table[i * slots + s] = jnp.where(s < count, at, nothing)
            entry = landed[i, s]
            high = entry.astype(BF16)
            upper[i, s * block : (s + 1) * block] = high
            lower[i, s * block : (s + 1) * block] = (
                entry - high.astype(F32)
            ).astype(BF16)

    def advance(step, x, y):
        i = x * cy + y
        field = fields[step % 2]
        lhs = jnp.concatenate(
            [
                field[jnp.minimum(jnp.maximum(table[i * slots + s], 0), nothing)]
                for s in range(slots)
            ],
            axis=1,
        )
        rhs = jnp.concatenate([upper[i], lower[i]], axis=1)
        product = jnp.dot(lhs, rhs, preferred_element_type=F32)
        value = product[:width, :block] + (
            product[width:, :block] + product[:width, block:] + product[width:, block:]
        )
        if step:
            value = 2.0 * value - vectors[step - 1][x, y]
        vectors[step + 1][x, y] = value
        if step + 1 < STEPS:
            put(fields[(step + 1) % 2], (x + 1) * pitch + y + 1, value)
        start_vector = v0[x, y]
        first_re, first_im = start_vector[:half], start_vector[half:]
        other_re, other_im = value[:half], value[half:]
        return (
            first_re * other_re + first_im * other_im,
            first_re * other_im - first_im * other_re,
        )

    def run(step, place, first, count, unroll):
        def body(k):
            cells = [place(first + k * unroll + u) for u in range(unroll)]
            if step == 0:
                for x, y in cells:
                    landing(x, y).wait()
            found = []
            for x, y in cells:
                if step == 0:
                    prepare(x, y)
                found.append(advance(step, x, y))
            low = step * width
            sums[low : low + half] += sum(real for real, _ in found)
            sums[low + half : low + width] += sum(imag for _, imag in found)

        if count == unroll:
            body(0)
        else:
            pl.loop(0, count // unroll)(body)

    for y in wire:
        start(x_copies(0, y))
    start(y_middles(0) + y_ends(0, 0) + y_ends(0, 1))
    sums[...] = jnp.zeros_like(sums)
    for field in fields:
        field[nothing] = jnp.zeros_like(field[nothing])
    row = lax.broadcasted_iota(jnp.int32, (16, block), 0)

    def crossing(at, me, size):
        low = (at == 0) & (me == 0)
        high = (at == 2) & (me == size - 1)
        return jnp.where(low, -1.0, jnp.where(high, 1.0, 0.0)).astype(F32)

    angle = kpoint[0] * crossing(row // 3, me_x, size_x)
    angle = angle + kpoint[1] * crossing(row % 3, me_y, size_y)
    turns[0], turns[1] = jnp.cos(angle), jnp.sin(angle)
    load_v0.wait()

    @pl.loop(0, cx * cy)
    def _(k):
        x, y = k // cy, k % cy
        put(field_a, (x + 1) * pitch + y + 1, v0[x, y])

    for step in range(STEPS):
        more = step + 1 < STEPS
        order = [mirror(step, y) for y in wire]
        near = 1 if step % 2 else 0
        run(step, interior, 0, early, 4)
        arrive(x_copies(step, order[0]))
        start(corner_copies(step, 1 - near))
        run(step, interior, early, inner - early, 4)
        arrive(x_copies(step, order[1]))
        start(corner_copies(step, near))
        put_x(step, order[0])
        put_x(step, order[1])
        arrive(y_middles(step) + y_ends(step, 0) + y_ends(step, 1))
        for side in range(2):

            @pl.loop(0, cx)
            def _(x):
                put_y(step, side, x + 1, 1)

        run(step, rim_y, 0, 2 * (cx - 2), 4)
        if more:
            start(y_middles(step + 1))
        for group, ys in enumerate(ready):
            arrive(x_copies(step, order[group + 2]))
            put_x(step, order[group + 2])
            if group < 2:
                side = 1 - near if group == 0 else near
                arrive(corner_copies(step, side))
                for end in range(2):
                    put_y(step, side, end * (cx + 1), 2 * end)
            run(step, rim_x(step, ys), 0, 2 * len(ys), 2 * len(ys))
            if more:
                if len(ys) > 1:
                    ys = ys[::-1]
                for y in ys:
                    start(x_copies(step + 1, mirror(step, y)))
                if group < 2:
                    start(y_ends(step + 1, 1 if mirror(step, ys[0]) == 0 else 0))

    found = lax.dot_general(
        jnp.ones((8, block), F32),
        sums[...],
        (((1,), (1,)), ((), ())),
        precision=lax.Precision.HIGHEST,
        preferred_element_type=F32,
    )[0:1]
    for name, size, me, ring, sent, got in (
        (name_x, size_x, me_x, ring_x, sum_send_x, sum_recv_x),
        (name_y, size_y, me_y, ring_y, sum_send_y, sum_recv_y),
    ):
        ring[me] = found
        copies = [
            pltpu.make_async_remote_copy(
                src_ref=ring.at[me],
                dst_ref=ring.at[me],
                send_sem=sent.at[j],
                recv_sem=got.at[j],
                device_id={name: lax.rem(me + j, size)},
                device_id_type=MESH,
            )
            for j in range(1, size)
        ]
        start(copies)
        for copy in copies:
            copy.wait()
        found = ring[0]
        for j in range(1, size):
            found = found + ring[j]
    total[...] = found
    for step in range(STEPS):
        for y in wire:
            for copy in x_copies(step, y):
                copy.wait_send()
        for side in range(2):
            for copy in y_ends(step, side) + corner_copies(step, side):
                copy.wait_send()
        for copy in y_middles(step):
            copy.wait_send()


def shards(axes, probes, pair_blocks, partners, shifts, counts, kpoint):
    (name_x, size_x), (name_y, size_y) = axes
    cx, cy, width, block = probes.shape
    slots = pair_blocks.shape[2]
    cells = cx * cy
    total_x, total_y = cx * size_x, cy * size_y
    rows = STEPS * width
    halo = (width, block)
    smem = pl.BlockSpec(memory_space=pltpu.SMEM)
    anywhere = pl.BlockSpec(memory_space=pl.ANY)
    vmem = pl.BlockSpec(memory_space=pltpu.VMEM)
    dma = pltpu.SemaphoreType.DMA
    kinds = 2 * cy + 10
    last, found = pl.pallas_call(
        functools.partial(kernel, axes),
        out_shape=(
            jax.ShapeDtypeStruct(probes.shape, F32),
            jax.ShapeDtypeStruct((1, rows), F32),
        ),
        in_specs=[smem, smem, smem, anywhere, anywhere],
        out_specs=(vmem, vmem),
        scratch_shapes=[
            pltpu.VMEM(probes.shape, F32),
            pltpu.VMEM(probes.shape, F32),
            pltpu.VMEM(probes.shape, F32),
            pltpu.VMEM((STEPS, 2, cy) + halo, F32),
            pltpu.VMEM((STEPS, 2, cx + 2) + halo, F32),
            pltpu.VMEM(((cx + 2) * (cy + 2) + 1, 2 * width, block), BF16),
            pltpu.VMEM(((cx + 2) * (cy + 2) + 1, 2 * width, block), BF16),
            pltpu.VMEM((cells, slots, block, block), F32),
            pltpu.VMEM((cells, slots * block, block), BF16),
            pltpu.VMEM((cells, slots * block, block), BF16),
            pltpu.VMEM((rows, block), F32),
            pltpu.VMEM((size_x, 1, rows), F32),
            pltpu.VMEM((size_y, 1, rows), F32),
            pltpu.SMEM((cells * slots,), jnp.int32),
            pltpu.VMEM((2, 16, block), F32),
            dma(()),
            dma((cells,)),
            dma((STEPS, kinds)),
            dma((STEPS, kinds)),
            dma((size_x,)),
            dma((size_x,)),
            dma((size_y,)),
            dma((size_y,)),
        ],
        compiler_params=pltpu.CompilerParams(
            collective_id=0, has_side_effects=True, vmem_limit_bytes=66_000_000
        ),
    )(partners, counts, kpoint, probes, pair_blocks)
    scale = 1.0 / math.sqrt(total_x * total_y * block)
    return last, (found[0] * scale).reshape(STEPS, 2, width // 2)


def solution(mesh):
    placed = (
        P("gx", "gy", None, None),
        P("gx", "gy", None, None, None),
        P("gx", "gy", None),
        P(None, "gx", "gy", None),
        P("gx", "gy"),
        P(),
    )
    axes = tuple((name, mesh.shape[name]) for name in ("gx", "gy"))
    return jax.shard_map(
        functools.partial(shards, axes),
        mesh=mesh,
        in_specs=placed,
        out_specs=(P("gx", "gy", None, None), P()),
        check_vma=False,
    )
```

```python
import functools
import math

import jax
import jax.numpy as jnp
from jax import lax
from jax.experimental import pallas as pl
from jax.experimental.pallas import tpu as pltpu
from jax.sharding import PartitionSpec as P

STEPS = 3
MESH = pl.DeviceIdType.MESH
F32, BF16 = jnp.float32, jnp.bfloat16


def kernel(
    axes, partners_hbm, counts_hbm, kpoint_hbm, v0_hbm, blocks_hbm, last, total,
    partners, counts, kpoint, v0, v1, v2, halo_x, halo_y, field_a, field_b, landed, upper, lower, sums, ring_x, ring_y, table, turns,
    v0_sem, small_sem, land_sem, send_sem, recv_sem, sum_send_x, sum_recv_x, sum_send_y, sum_recv_y,
):
    (name_x, size_x), (name_y, size_y) = axes
    cx, cy, width, block = v0.shape
    slots = landed.shape[1]
    half = width // 2
    pitch = cy + 2
    nothing = (cx + 2) * pitch
    me_x, me_y = lax.axis_index(name_x), lax.axis_index(name_y)
    total_x, total_y = cx * size_x, cy * size_y
    vectors = (v0, v1, v2, last)
    fields = (field_a, field_b)

    def landing(x, y):
        i = x * cy + y
        return pltpu.make_async_copy(blocks_hbm.at[x, y], landed.at[i], land_sem.at[i])

    inner = (cx - 2) * (cy - 2)

    def interior(k):
        return 1 + k // (cy - 2), 1 + k % (cy - 2)

    def rim_y(k):
        return 1 + k // 2, (k % 2) * (cy - 1)

    def mirror(step, y):
        return cy - 1 - y if step % 2 else y

    def rim_x(step, ys):
        return lambda k: ((k % 2) * (cx - 1), mirror(step, ys[k // 2]))

    wire = (0, cy - 1, cy - 2) + tuple(range(1, cy - 2))
    ready = ((cy - 1,), (0,)) + tuple((p - 1,) for p in range(2, cy - 3))
    ready = ready + ((cy - 4, cy - 3, cy - 2),)
    early = inner // 2

    for signal_name, size, me in ((name_x, size_x, me_x), (name_y, size_y, me_y)):
        for j in range(1, size):
            pl.semaphore_signal(
                pltpu.get_barrier_semaphore(),
                inc=1,
                device_id={signal_name: lax.rem(me + j, size)},
                device_id_type=MESH,
            )
    load_v0 = pltpu.make_async_copy(v0_hbm, v0, v0_sem)
    load_v0.start()
    small = [
        pltpu.make_async_copy(there, here, small_sem.at[i])
        for i, (there, here) in enumerate(
            ((partners_hbm, partners), (counts_hbm, counts), (kpoint_hbm, kpoint))
        )
    ]
    for copy in small:
        copy.start()
    for place, count in (
        (interior, inner),
        (rim_y, 2 * (cx - 2)),
        *((rim_x(0, ys), 2 * len(ys)) for ys in ready),
    ):
        if count > 6:

            @pl.loop(0, count)
            def _(k):
                landing(*place(k)).start()
        else:
            for k in range(count):
                landing(*place(k)).start()
    pl.semaphore_wait(pltpu.get_barrier_semaphore(), size_x + size_y - 2)

    def towards(name, size, me, side):
        return {name: lax.rem(me + (size - 1 if side else 1), size)}

    def remote(step, kind, src, dst, peer):
        return pltpu.make_async_remote_copy(
            src_ref=src,
            dst_ref=dst,
            send_sem=send_sem.at[step, kind],
            recv_sem=recv_sem.at[step, kind],
            device_id=peer,
            device_id_type=MESH,
        )

    def source(step):
        return vectors[step] if step else v0_hbm

    def x_copies(step, y):
        return [
            remote(
                step,
                2 * y + side,
                source(step).at[0 if side else cx - 1, y],
                halo_x.at[step, side, y],
                towards(name_x, size_x, me_x, side),
            )
            for side in range(2)
        ]

    def y_copy(step, side, x, length):
        return remote(
            step,
            2 * cy + 3 * side + (0 if x == 0 else 1 if x == 1 else 2),
            source(step).at[pl.ds(x, length), 0 if side else cy - 1],
            halo_y.at[step, side, pl.ds(1 + x, length)],
            towards(name_y, size_y, me_y, side),
        )

    def y_middles(step):
        return [y_copy(step, side, 1, cx - 2) for side in range(2)]

    def y_ends(step, side):
        return [y_copy(step, side, x, 1) for x in (0, cx - 1)]

    def corner_copies(step, side):
        return [
            remote(
                step,
                2 * cy + 6 + 2 * side + end,
                halo_x.at[step, end, 0 if side else cy - 1],
                halo_y.at[step, side, end * (cx + 1)],
                towards(name_y, size_y, me_y, side),
            )
            for end in range(2)
        ]

    def start(copies):
        for copy in copies:
            copy.start()

    def arrive(copies):
        for copy in copies:
            copy.wait_recv()

    def put(field, position, value):
        high = value.astype(BF16)
        field[position, :width] = high
        field[position, width:] = (value - high.astype(F32)).astype(BF16)

    def put_turned(field, position, value, at_x, at_y):
        entry = at_x * 3 + at_y
        cosine, sine = turns[0, entry : entry + 1], turns[1, entry : entry + 1]
        real, imag = value[:half], value[half:]
        put(
            field,
            position,
            jnp.concatenate(
                [cosine * real - sine * imag, sine * real + cosine * imag], axis=0
            ),
        )

    def put_x(step, y):
        for side in range(2):
            put_turned(
                fields[step % 2],
                side * (cx + 1) * pitch + y + 1,
                halo_x[step, side, y],
                2 * side,
                1,
            )

    def put_y(step, side, x, at_x):
        put_turned(
            fields[step % 2],
            x * pitch + side * (cy + 1),
            halo_y[step, side, x],
            at_x,
            2 * side,
        )

    def prepare(x, y):
        i = x * cy + y
        count = counts[x, y]
        for s in range(slots):
            partner = partners[x, y, s]
            partner_x = (partner * (((1 << 20) + total_y - 1) // total_y)) >> 20
            at_x = partner_x - me_x * cx + 1
            at_x = jnp.where(at_x < 0, at_x + total_x, at_x)
            at_x = jnp.where(at_x >= total_x, at_x - total_x, at_x)
            at_y = partner - partner_x * total_y - me_y * cy + 1
            at_y = jnp.where(at_y < 0, at_y + total_y, at_y)
            at_y = jnp.where(at_y >= total_y, at_y - total_y, at_y)
            at = jnp.minimum(jnp.maximum(at_x * pitch + at_y, 0), nothing - 1)
            table[i * slots + s] = jnp.where(s < count, at, nothing)
            entry = landed[i, s]
            high = entry.astype(BF16)
            upper[i, s * block : (s + 1) * block] = high
            lower[i, s * block : (s + 1) * block] = (
                entry - high.astype(F32)
            ).astype(BF16)

    def advance(step, x, y):
        i = x * cy + y
        field = fields[step % 2]
        lhs = jnp.concatenate(
            [
                field[jnp.minimum(jnp.maximum(table[i * slots + s], 0), nothing)]
                for s in range(slots)
            ],
            axis=1,
        )
        rhs = jnp.concatenate([upper[i], lower[i]], axis=1)
        product = jnp.dot(lhs, rhs, preferred_element_type=F32)
        value = product[:width, :block] + (
            product[width:, :block] + product[:width, block:] + product[width:, block:]
        )
        if step:
            value = 2.0 * value - vectors[step - 1][x, y]
        vectors[step + 1][x, y] = value
        if step + 1 < STEPS:
            put(fields[(step + 1) % 2], (x + 1) * pitch + y + 1, value)
        start_vector = v0[x, y]
        first_re, first_im = start_vector[:half], start_vector[half:]
        other_re, other_im = value[:half], value[half:]
        return (
            first_re * other_re + first_im * other_im,
            first_re * other_im - first_im * other_re,
        )

    def run(step, place, first, count, unroll):
        def body(k):
            cells = [place(first + k * unroll + u) for u in range(unroll)]
            if step == 0:
                for x, y in cells:
                    landing(x, y).wait()
            found = []
            for x, y in cells:
                if step == 0:
                    prepare(x, y)
                found.append(advance(step, x, y))
            low = step * width
            sums[low : low + half] += sum(real for real, _ in found)
            sums[low + half : low + width] += sum(imag for _, imag in found)

        if count == unroll:
            body(0)
        else:
            pl.loop(0, count // unroll)(body)

    for y in wire:
        start(x_copies(0, y))
    start(y_middles(0) + y_ends(0, 0) + y_ends(0, 1))
    sums[...] = jnp.zeros_like(sums)
    for field in fields:
        field[nothing] = jnp.zeros_like(field[nothing])
    row = lax.broadcasted_iota(jnp.int32, (16, block), 0)
    for copy in small:
        copy.wait()

    def crossing(at, me, size):
        low = (at == 0) & (me == 0)
        high = (at == 2) & (me == size - 1)
        return jnp.where(low, -1.0, jnp.where(high, 1.0, 0.0)).astype(F32)

    angle = kpoint[0] * crossing(row // 3, me_x, size_x)
    angle = angle + kpoint[1] * crossing(row % 3, me_y, size_y)
    turns[0], turns[1] = jnp.cos(angle), jnp.sin(angle)
    load_v0.wait()

    @pl.loop(0, cx * cy)
    def _(k):
        x, y = k // cy, k % cy
        put(field_a, (x + 1) * pitch + y + 1, v0[x, y])

    for step in range(STEPS):
        more = step + 1 < STEPS
        order = [mirror(step, y) for y in wire]
        near = 1 if step % 2 else 0
        run(step, interior, 0, early, 4)
        arrive(x_copies(step, order[0]))
        start(corner_copies(step, 1 - near))
        run(step, interior, early, inner - early, 4)
        arrive(x_copies(step, order[1]))
        start(corner_copies(step, near))
        put_x(step, order[0])
        put_x(step, order[1])
        arrive(y_middles(step) + y_ends(step, 0) + y_ends(step, 1))
        for side in range(2):

            @pl.loop(0, cx)
            def _(x):
                put_y(step, side, x + 1, 1)

        run(step, rim_y, 0, 2 * (cx - 2), 4)
        if more:
            start(y_middles(step + 1))
        for group, ys in enumerate(ready):
            arrive(x_copies(step, order[group + 2]))
            put_x(step, order[group + 2])
            if group < 2:
                side = 1 - near if group == 0 else near
                arrive(corner_copies(step, side))
                for end in range(2):
                    put_y(step, side, end * (cx + 1), 2 * end)
            run(step, rim_x(step, ys), 0, 2 * len(ys), 2 * len(ys))
            if more:
                if len(ys) > 1:
                    ys = ys[::-1]
                for y in ys:
                    start(x_copies(step + 1, mirror(step, y)))
                if group < 2:
                    start(y_ends(step + 1, 1 if mirror(step, ys[0]) == 0 else 0))

    found = lax.dot_general(
        jnp.ones((8, block), F32),
        sums[...],
        (((1,), (1,)), ((), ())),
        precision=lax.Precision.HIGHEST,
        preferred_element_type=F32,
    )[0:1]
    for name, size, me, ring, sent, got in (
        (name_x, size_x, me_x, ring_x, sum_send_x, sum_recv_x),
        (name_y, size_y, me_y, ring_y, sum_send_y, sum_recv_y),
    ):
        ring[me] = found
        copies = [
            pltpu.make_async_remote_copy(
                src_ref=ring.at[me],
                dst_ref=ring.at[me],
                send_sem=sent.at[j],
                recv_sem=got.at[j],
                device_id={name: lax.rem(me + j, size)},
                device_id_type=MESH,
            )
            for j in range(1, size)
        ]
        start(copies)
        for copy in copies:
            copy.wait()
        found = ring[0]
        for j in range(1, size):
            found = found + ring[j]
    total[...] = found
    for step in range(STEPS):
        for y in wire:
            for copy in x_copies(step, y):
                copy.wait_send()
        for side in range(2):
            for copy in y_ends(step, side) + corner_copies(step, side):
                copy.wait_send()
        for copy in y_middles(step):
            copy.wait_send()


def finish(scale, last, found, out, total, sem):
    copies = [
        pltpu.make_async_copy(last.at[x], out.at[x], sem.at[x])
        for x in range(last.shape[0])
    ]
    for copy in copies:
        copy.start()
    half = total.shape[2]
    for step in range(STEPS):
        for part in range(2):
            low = (2 * step + part) * half
            total[step, part : part + 1] = found[:, low : low + half] * scale
    for copy in copies:
        copy.wait()


def shards(axes, probes, pair_blocks, partners, shifts, counts, kpoint):
    (name_x, size_x), (name_y, size_y) = axes
    cx, cy, width, block = probes.shape
    slots = pair_blocks.shape[2]
    cells = cx * cy
    total_x, total_y = cx * size_x, cy * size_y
    rows = STEPS * width
    halo = (width, block)
    hbm = pl.BlockSpec(memory_space=pltpu.HBM)
    vmem = pl.BlockSpec(memory_space=pltpu.VMEM)
    dma = pltpu.SemaphoreType.DMA
    kinds = 2 * cy + 10
    last, found = pl.pallas_call(
        functools.partial(kernel, axes),
        out_shape=(
            pltpu.VMEM(probes.shape, F32),
            pltpu.VMEM((1, rows), F32),
        ),
        in_specs=[hbm] * 5,
        out_specs=(vmem, vmem),
        scratch_shapes=[
            pltpu.SMEM(partners.shape, jnp.int32),
            pltpu.SMEM(counts.shape, jnp.int32),
            pltpu.SMEM(kpoint.shape, F32),
            pltpu.VMEM(probes.shape, F32),
            pltpu.VMEM(probes.shape, F32),
            pltpu.VMEM(probes.shape, F32),
            pltpu.VMEM((STEPS, 2, cy) + halo, F32),
            pltpu.VMEM((STEPS, 2, cx + 2) + halo, F32),
            pltpu.VMEM(((cx + 2) * (cy + 2) + 1, 2 * width, block), BF16),
            pltpu.VMEM(((cx + 2) * (cy + 2) + 1, 2 * width, block), BF16),
            pltpu.VMEM((cells, slots, block, block), F32),
            pltpu.VMEM((cells, slots * block, block), BF16),
            pltpu.VMEM((cells, slots * block, block), BF16),
            pltpu.VMEM((rows, block), F32),
            pltpu.VMEM((size_x, 1, rows), F32),
            pltpu.VMEM((size_y, 1, rows), F32),
            pltpu.SMEM((cells * slots,), jnp.int32),
            pltpu.VMEM((2, 16, block), F32),
            dma(()),
            dma((3,)),
            dma((cells,)),
            dma((STEPS, kinds)),
            dma((STEPS, kinds)),
            dma((size_x,)),
            dma((size_x,)),
            dma((size_y,)),
            dma((size_y,)),
        ],
        compiler_params=pltpu.CompilerParams(
            collective_id=0, has_side_effects=True, vmem_limit_bytes=60_000_000
        ),
    )(partners, counts, kpoint, probes, pair_blocks)
    scale = 1.0 / math.sqrt(total_x * total_y * block)
    return pl.pallas_call(
        functools.partial(finish, scale),
        out_shape=(
            jax.ShapeDtypeStruct(probes.shape, F32),
            jax.ShapeDtypeStruct((STEPS, 2, width // 2), F32),
        ),
        in_specs=[vmem, vmem],
        out_specs=(hbm, vmem),
        scratch_shapes=[dma((cx,))],
    )(*(pltpu.with_memory_space_constraint(part, pltpu.VMEM) for part in (last, found)))


def solution(mesh):
    placed = (
        P("gx", "gy", None, None),
        P("gx", "gy", None, None, None),
        P("gx", "gy", None),
        P(None, "gx", "gy", None),
        P("gx", "gy"),
        P(),
    )
    axes = tuple((name, mesh.shape[name]) for name in ("gx", "gy"))
    return jax.shard_map(
        functools.partial(shards, axes),
        mesh=mesh,
        in_specs=placed,
        out_specs=(P("gx", "gy", None, None), P()),
        check_vma=False,
    )
```

```python
import functools
import math

import jax
import jax.numpy as jnp
from jax import lax
from jax.experimental import pallas as pl
from jax.experimental.pallas import tpu as pltpu
from jax.sharding import PartitionSpec as P

STEPS = 3
MESH = pl.DeviceIdType.MESH
F32, BF16 = jnp.float32, jnp.bfloat16


def kernel(
    axes, partners_hbm, counts_hbm, kpoint_hbm, v0_hbm, blocks_hbm, last, total,
    partners, counts, kpoint, v0, v1, v2, halo_x, halo_y, field_a, field_b, landed, upper, lower, sums, ring_x, ring_y, table, sooner, late, turns,
    v0_sem, small_sem, land_sem, send_sem, recv_sem, sum_send_x, sum_recv_x, sum_send_y, sum_recv_y,
):
    (name_x, size_x), (name_y, size_y) = axes
    cx, cy, width, block = v0.shape
    slots = landed.shape[1]
    half = width // 2
    pitch = cy + 2
    nothing = (cx + 2) * pitch
    me_x, me_y = lax.axis_index(name_x), lax.axis_index(name_y)
    total_x, total_y = cx * size_x, cy * size_y
    vectors = (v0, v1, v2, last)
    fields = (field_a, field_b)

    def landing(x, y):
        i = x * cy + y
        return pltpu.make_async_copy(blocks_hbm.at[x, y], landed.at[i], land_sem.at[i])

    inner = (cx - 2) * (cy - 2)

    def interior(k):
        return 1 + k // (cy - 2), 1 + k % (cy - 2)

    def rim_y(k):
        return 1 + k // 2, (k % 2) * (cy - 1)

    def mirror(step, y):
        return cy - 1 - y if step % 2 else y

    def rim_x(step, ys):
        return lambda k: ((k % 2) * (cx - 1), mirror(step, ys[k // 2]))

    wire = (0, cy - 1, cy - 2) + tuple(range(1, cy - 2))
    ready = ((cy - 1,), (0,)) + tuple((p - 1,) for p in range(2, cy - 3))
    ready = ready + ((cy - 4, cy - 3, cy - 2),)
    final = [rim_x(STEPS - 1, ready[-1])(k) for k in range(2 * len(ready[-1]))]
    final_y = mirror(STEPS - 1, wire[-1])
    early = inner // 2

    for signal_name, size, me in ((name_x, size_x, me_x), (name_y, size_y, me_y)):
        for j in range(1, size):
            pl.semaphore_signal(
                pltpu.get_barrier_semaphore(),
                inc=1,
                device_id={signal_name: lax.rem(me + j, size)},
                device_id_type=MESH,
            )
    load_v0 = pltpu.make_async_copy(v0_hbm, v0, v0_sem)
    load_v0.start()
    small = [
        pltpu.make_async_copy(there, here, small_sem.at[i])
        for i, (there, here) in enumerate(
            ((partners_hbm, partners), (counts_hbm, counts), (kpoint_hbm, kpoint))
        )
    ]
    for copy in small:
        copy.start()
    for place, count in (
        (interior, inner),
        (rim_y, 2 * (cx - 2)),
        *((rim_x(0, ys), 2 * len(ys)) for ys in ready),
    ):
        if count > 6:

            @pl.loop(0, count)
            def _(k):
                landing(*place(k)).start()
        else:
            for k in range(count):
                landing(*place(k)).start()
    pl.semaphore_wait(pltpu.get_barrier_semaphore(), size_x + size_y - 2)

    def towards(name, size, me, side):
        return {name: lax.rem(me + (size - 1 if side else 1), size)}

    def remote(step, kind, src, dst, peer):
        return pltpu.make_async_remote_copy(
            src_ref=src,
            dst_ref=dst,
            send_sem=send_sem.at[step, kind],
            recv_sem=recv_sem.at[step, kind],
            device_id=peer,
            device_id_type=MESH,
        )

    def source(step):
        return vectors[step] if step else v0_hbm

    def x_copies(step, y):
        return [
            remote(
                step,
                2 * y + side,
                source(step).at[0 if side else cx - 1, y],
                halo_x.at[step, side, y],
                towards(name_x, size_x, me_x, side),
            )
            for side in range(2)
        ]

    def y_copy(step, side, x, length):
        return remote(
            step,
            2 * cy + 3 * side + (0 if x == 0 else 1 if x == 1 else 2),
            source(step).at[pl.ds(x, length), 0 if side else cy - 1],
            halo_y.at[step, side, pl.ds(1 + x, length)],
            towards(name_y, size_y, me_y, side),
        )

    def y_middles(step):
        return [y_copy(step, side, 1, cx - 2) for side in range(2)]

    def y_ends(step, side):
        return [y_copy(step, side, x, 1) for x in (0, cx - 1)]

    def corner_copies(step, side):
        return [
            remote(
                step,
                2 * cy + 6 + 2 * side + end,
                halo_x.at[step, end, 0 if side else cy - 1],
                halo_y.at[step, side, end * (cx + 1)],
                towards(name_y, size_y, me_y, side),
            )
            for end in range(2)
        ]

    def start(copies):
        for copy in copies:
            copy.start()

    def arrive(copies):
        for copy in copies:
            copy.wait_recv()

    def row_sums(first, length):
        return lax.dot_general(
            jnp.ones((8, block), F32),
            sums[first : first + length],
            (((1,), (1,)), ((), ())),
            precision=lax.Precision.HIGHEST,
            preferred_element_type=F32,
        )[0:1]

    def put(field, position, value):
        high = value.astype(BF16)
        field[position, :width] = high
        field[position, width:] = (value - high.astype(F32)).astype(BF16)

    def put_turned(field, position, value, at_x, at_y):
        entry = at_x * 3 + at_y
        cosine, sine = turns[0, entry : entry + 1], turns[1, entry : entry + 1]
        real, imag = value[:half], value[half:]
        put(
            field,
            position,
            jnp.concatenate(
                [cosine * real - sine * imag, sine * real + cosine * imag], axis=0
            ),
        )

    def put_x(step, y):
        for side in range(2):
            put_turned(
                fields[step % 2],
                side * (cx + 1) * pitch + y + 1,
                halo_x[step, side, y],
                2 * side,
                1,
            )

    def put_y(step, side, x, at_x):
        put_turned(
            fields[step % 2],
            x * pitch + side * (cy + 1),
            halo_y[step, side, x],
            at_x,
            2 * side,
        )

    def prepare(x, y):
        i = x * cy + y
        count = counts[x, y]
        closing = isinstance(y, int) and (x, y) in final
        late_slot, late_place = jnp.int32(0), jnp.int32(nothing)
        from_x = lax.rem(me_x * cx + total_x - 1, total_x)
        from_y = lax.rem(me_y * cy + total_y - 1, total_y)
        for s in range(slots):
            partner = partners[x, y, s]
            partner_x = (partner * (((1 << 20) + total_y - 1) // total_y)) >> 20
            at_x = partner_x - from_x
            at_x = jnp.where(at_x < 0, at_x + total_x, at_x)
            at_y = partner - partner_x * total_y - from_y
            at_y = jnp.where(at_y < 0, at_y + total_y, at_y)
            at = jnp.where(s < count, at_x * pitch + at_y, nothing)
            table[i * slots + s] = at
            if closing:
                k = final.index((x, y))
                late_at = (0 if x == 0 else cx + 1) * pitch + final_y + 1
                is_late = at == late_at
                sooner[k * slots + s] = jnp.where(is_late, nothing, at)
                late_slot = jnp.where(is_late, s, late_slot)
                late_place = jnp.where(is_late, late_at, late_place)
            entry = landed[i, s]
            high = entry.astype(BF16)
            upper[i, s] = high
            lower[i, s] = (
                entry - high.astype(F32)
            ).astype(BF16)
        if closing:
            k = final.index((x, y))
            late[2 * k], late[2 * k + 1] = late_slot, late_place

    def split_dot(lhs, rhs):
        product = jnp.dot(lhs, rhs, preferred_element_type=F32)
        return product[:width, :block] + (
            product[width:, :block] + product[:width, block:] + product[width:, block:]
        )

    def gathered(step, x, y, entries, first):
        i = x * cy + y
        field = fields[step % 2]
        lhs = jnp.concatenate(
            [
                field[jnp.minimum(jnp.maximum(entries[first + s], 0), nothing)]
                for s in range(slots)
            ],
            axis=1,
        )
        high = upper[i].reshape(slots * block, block)
        low = lower[i].reshape(slots * block, block)
        value = split_dot(lhs, jnp.concatenate([high, low], axis=1))
        return 2.0 * value - vectors[step - 1][x, y] if step else value

    def meet(x, y, value):
        start_vector = v0[x, y]
        first_re, first_im = start_vector[:half], start_vector[half:]
        other_re, other_im = value[:half], value[half:]
        return (
            first_re * other_re + first_im * other_im,
            first_re * other_im - first_im * other_re,
        )

    def add_up(step, found):
        low = step * width
        sums[low : low + half] += sum(real for real, _ in found)
        sums[low + half : low + width] += sum(imag for _, imag in found)

    def advance(step, x, y):
        value = gathered(step, x, y, table, (x * cy + y) * slots)
        vectors[step + 1][x, y] = value
        if step + 1 < STEPS:
            put(fields[(step + 1) % 2], (x + 1) * pitch + y + 1, value)
        return meet(x, y, value)

    def sooner_part():
        for k, (x, y) in enumerate(final):
            last[x, y] = gathered(STEPS - 1, x, y, sooner, k * slots)

    def late_part():
        found = []
        field = fields[(STEPS - 1) % 2]
        for k, (x, y) in enumerate(final):
            i = x * cy + y
            slot = jnp.minimum(jnp.maximum(late[2 * k], 0), slots - 1)
            place = jnp.minimum(jnp.maximum(late[2 * k + 1], 0), nothing)
            rhs = jnp.concatenate([upper[i, slot], lower[i, slot]], axis=1)
            value = last[x, y] + 2.0 * split_dot(field[place], rhs)
            last[x, y] = value
            found.append(meet(x, y, value))
        add_up(STEPS - 1, found)

    def run(step, place, first, count, unroll):
        def body(k):
            cells = [place(first + k * unroll + u) for u in range(unroll)]
            if step == 0:
                for x, y in cells:
                    landing(x, y).wait()
            found = []
            for x, y in cells:
                if step == 0:
                    prepare(x, y)
                found.append(advance(step, x, y))
            add_up(step, found)

        if count == unroll:
            body(0)
        else:
            pl.loop(0, count // unroll)(body)

    for y in wire:
        start(x_copies(0, y))
    start(y_middles(0) + y_ends(0, 0) + y_ends(0, 1))
    sums[...] = jnp.zeros_like(sums)
    for field in fields:
        field[nothing] = jnp.zeros_like(field[nothing])
    row = lax.broadcasted_iota(jnp.int32, (16, block), 0)
    for copy in small:
        copy.wait()

    def crossing(at, me, size):
        low = (at == 0) & (me == 0)
        high = (at == 2) & (me == size - 1)
        return jnp.where(low, -1.0, jnp.where(high, 1.0, 0.0)).astype(F32)

    angle = kpoint[0] * crossing(row // 3, me_x, size_x)
    angle = angle + kpoint[1] * crossing(row % 3, me_y, size_y)
    turns[0], turns[1] = jnp.cos(angle), jnp.sin(angle)
    load_v0.wait()

    @pl.loop(0, cx * cy)
    def _(k):
        x, y = k // cy, k % cy
        put(field_a, (x + 1) * pitch + y + 1, v0[x, y])

    for step in range(STEPS):
        more = step + 1 < STEPS
        order = [mirror(step, y) for y in wire]
        near = 1 if step % 2 else 0
        run(step, interior, 0, early, 4)
        arrive(x_copies(step, order[0]))
        start(corner_copies(step, 1 - near))
        run(step, interior, early, inner - early, 4)
        arrive(x_copies(step, order[1]))
        start(corner_copies(step, near))
        put_x(step, order[0])
        put_x(step, order[1])
        arrive(y_middles(step) + y_ends(step, 0) + y_ends(step, 1))
        for side in range(2):

            @pl.loop(0, cx)
            def _(x):
                put_y(step, side, x + 1, 1)

        run(step, rim_y, 0, 2 * (cx - 2), 4)
        if more:
            start(y_middles(step + 1))
        for group, ys in enumerate(ready):
            closing = not more and group + 1 == len(ready)
            if closing:
                sooner_part()
                ring_x[me_x, :, : step * width] = row_sums(0, step * width)
            arrive(x_copies(step, order[group + 2]))
            put_x(step, order[group + 2])
            if group < 2:
                side = 1 - near if group == 0 else near
                arrive(corner_copies(step, side))
                for end in range(2):
                    put_y(step, side, end * (cx + 1), 2 * end)
            if closing:
                late_part()
            else:
                run(step, rim_x(step, ys), 0, 2 * len(ys), 2 * len(ys))
            if more:
                if len(ys) > 1:
                    ys = ys[::-1]
                for y in ys:
                    start(x_copies(step + 1, mirror(step, y)))
                if group < 2:
                    start(y_ends(step + 1, 1 if mirror(step, ys[0]) == 0 else 0))

    low = (STEPS - 1) * width
    ring_x[me_x, :, low:] = row_sums(low, width)
    for name, size, me, ring, sent, got in (
        (name_x, size_x, me_x, ring_x, sum_send_x, sum_recv_x),
        (name_y, size_y, me_y, ring_y, sum_send_y, sum_recv_y),
    ):
        if ring is ring_y:
            ring[me] = found
        copies = [
            pltpu.make_async_remote_copy(
                src_ref=ring.at[me],
                dst_ref=ring.at[me],
                send_sem=sent.at[j],
                recv_sem=got.at[j],
                device_id={name: lax.rem(me + j, size)},
                device_id_type=MESH,
            )
            for j in range(1, size)
        ]
        start(copies)
        for copy in copies:
            copy.wait()
        found = ring[0]
        for j in range(1, size):
            found = found + ring[j]
    scale = 1.0 / math.sqrt(total_x * total_y * block)
    for part in range(2 * STEPS):
        total[part // 2, part % 2 : part % 2 + 1] = (
            found[:, part * half : (part + 1) * half] * scale
        )
    for step in range(STEPS):
        for y in wire:
            for copy in x_copies(step, y):
                copy.wait_send()
        for side in range(2):
            for copy in y_ends(step, side) + corner_copies(step, side):
                copy.wait_send()
        for copy in y_middles(step):
            copy.wait_send()


def finish(last, total, last_out, total_out, sem):
    cx = last.shape[0]
    copies = [
        pltpu.make_async_copy(last.at[x], last_out.at[x], sem.at[x]) for x in range(cx)
    ]
    copies.append(pltpu.make_async_copy(total, total_out, sem.at[cx]))
    for copy in copies:
        copy.start()
    for copy in copies:
        copy.wait()


def shards(axes, probes, pair_blocks, partners, shifts, counts, kpoint):
    (name_x, size_x), (name_y, size_y) = axes
    cx, cy, width, block = probes.shape
    slots = pair_blocks.shape[2]
    cells = cx * cy
    rows = STEPS * width
    halo = (width, block)
    hbm = pl.BlockSpec(memory_space=pltpu.HBM)
    vmem = pl.BlockSpec(memory_space=pltpu.VMEM)
    dma = pltpu.SemaphoreType.DMA
    kinds = 2 * cy + 10
    last, found = pl.pallas_call(
        functools.partial(kernel, axes),
        out_shape=(
            pltpu.VMEM(probes.shape, F32),
            pltpu.VMEM((STEPS, 2, width // 2), F32),
        ),
        in_specs=[hbm] * 5,
        out_specs=(vmem, vmem),
        scratch_shapes=[
            pltpu.SMEM(partners.shape, jnp.int32),
            pltpu.SMEM(counts.shape, jnp.int32),
            pltpu.SMEM(kpoint.shape, F32),
            pltpu.VMEM(probes.shape, F32),
            pltpu.VMEM(probes.shape, F32),
            pltpu.VMEM(probes.shape, F32),
            pltpu.VMEM((STEPS, 2, cy) + halo, F32),
            pltpu.VMEM((STEPS, 2, cx + 2) + halo, F32),
            pltpu.VMEM(((cx + 2) * (cy + 2) + 1, 2 * width, block), BF16),
            pltpu.VMEM(((cx + 2) * (cy + 2) + 1, 2 * width, block), BF16),
            pltpu.VMEM((cells, slots, block, block), F32),
            pltpu.VMEM((cells, slots, block, block), BF16),
            pltpu.VMEM((cells, slots, block, block), BF16),
            pltpu.VMEM((rows, block), F32),
            pltpu.VMEM((size_x, 1, rows), F32),
            pltpu.VMEM((size_y, 1, rows), F32),
            pltpu.SMEM((cells * slots,), jnp.int32),
            pltpu.SMEM((2 * cy * slots,), jnp.int32),
            pltpu.SMEM((4 * cy,), jnp.int32),
            pltpu.VMEM((2, 16, block), F32),
            dma(()),
            dma((3,)),
            dma((cells,)),
            dma((STEPS, kinds)),
            dma((STEPS, kinds)),
            dma((size_x,)),
            dma((size_x,)),
            dma((size_y,)),
            dma((size_y,)),
        ],
        compiler_params=pltpu.CompilerParams(
            collective_id=0, has_side_effects=True, vmem_limit_bytes=60_000_000
        ),
    )(partners, counts, kpoint, probes, pair_blocks)
    return pl.pallas_call(
        finish,
        out_shape=(
            jax.ShapeDtypeStruct(probes.shape, F32),
            jax.ShapeDtypeStruct((STEPS, 2, width // 2), F32),
        ),
        in_specs=[vmem, vmem],
        out_specs=(hbm, hbm),
        scratch_shapes=[dma((cx + 1,))],
    )(*(pltpu.with_memory_space_constraint(part, pltpu.VMEM) for part in (last, found)))


def solution(mesh):
    placed = (
        P("gx", "gy", None, None),
        P("gx", "gy", None, None, None),
        P("gx", "gy", None),
        P(None, "gx", "gy", None),
        P("gx", "gy"),
        P(),
    )
    axes = tuple((name, mesh.shape[name]) for name in ("gx", "gy"))
    return jax.shard_map(
        functools.partial(shards, axes),
        mesh=mesh,
        in_specs=placed,
        out_specs=(P("gx", "gy", None, None), P()),
        check_vma=False,
    )
```

```python
import functools
import math

import jax
import jax.numpy as jnp
from jax import lax
from jax.experimental import pallas as pl
from jax.experimental.pallas import tpu as pltpu
from jax.sharding import PartitionSpec as P

STEPS = 3
MESH = pl.DeviceIdType.MESH
F32, BF16 = jnp.float32, jnp.bfloat16


def kernel(
    axes, direct, partners_hbm, counts_hbm, kpoint_hbm, v0_hbm, blocks_hbm, last, total,
    partners, counts, kpoint, v0, v1, v2, halo_x, halo_y, field_a, field_b, landed, upper, lower, sums, gather, ring, table, sooner, late, turns,
    v0_sem, small_sem, land_sem, send_sem, recv_sem, sum_send, sum_recv,
):
    (name_x, size_x), (name_y, size_y) = axes
    cx, cy, width, block = v0.shape
    slots = landed.shape[1]
    half = width // 2
    pitch = cy + 2
    nothing = (cx + 2) * pitch
    me_x, me_y = lax.axis_index(name_x), lax.axis_index(name_y)
    total_x, total_y = cx * size_x, cy * size_y
    vectors = (v0, v1, v2, last)
    fields = (field_a, field_b)

    def landing(x, y):
        i = x * cy + y
        return pltpu.make_async_copy(blocks_hbm.at[x, y], landed.at[i], land_sem.at[i])

    inner = (cx - 2) * (cy - 2)

    def interior(k):
        return 1 + k // (cy - 2), 1 + k % (cy - 2)

    def rim_y(k):
        return 1 + k // 2, (k % 2) * (cy - 1)

    def mirror(step, y):
        return cy - 1 - y if step % 2 else y

    def rim_x(step, ys):
        return lambda k: ((k % 2) * (cx - 1), mirror(step, ys[k // 2]))

    wire = (0, cy - 1, cy - 2) + tuple(range(1, cy - 2))
    ready = ((cy - 1,), (0,)) + tuple((p - 1,) for p in range(2, cy - 3))
    ready = ready + ((cy - 4, cy - 3, cy - 2),)
    final = [rim_x(STEPS - 1, ready[-1])(k) for k in range(2 * len(ready[-1]))]
    final_y = mirror(STEPS - 1, wire[-1])
    early = inner // 2

    for signal_name, size, me in ((name_x, size_x, me_x), (name_y, size_y, me_y)):
        for j in range(1, size):
            pl.semaphore_signal(
                pltpu.get_barrier_semaphore(),
                inc=1,
                device_id={signal_name: lax.rem(me + j, size)},
                device_id_type=MESH,
            )
    load_v0 = pltpu.make_async_copy(v0_hbm, v0, v0_sem)
    load_v0.start()
    small = [
        pltpu.make_async_copy(there, here, small_sem.at[i])
        for i, (there, here) in enumerate(
            ((partners_hbm, partners), (counts_hbm, counts), (kpoint_hbm, kpoint))
        )
    ]
    for copy in small:
        copy.start()
    for place, count in (
        (interior, inner),
        (rim_y, 2 * (cx - 2)),
        *((rim_x(0, ys), 2 * len(ys)) for ys in ready),
    ):
        if count > 6:

            @pl.loop(0, count)
            def _(k):
                landing(*place(k)).start()
        else:
            for k in range(count):
                landing(*place(k)).start()
    pl.semaphore_wait(pltpu.get_barrier_semaphore(), size_x + size_y - 2)

    def towards(name, size, me, side):
        return {name: lax.rem(me + (size - 1 if side else 1), size)}

    def remote(step, kind, src, dst, peer):
        return pltpu.make_async_remote_copy(
            src_ref=src,
            dst_ref=dst,
            send_sem=send_sem.at[step, kind],
            recv_sem=recv_sem.at[step, kind],
            device_id=peer,
            device_id_type=MESH,
        )

    def source(step):
        return vectors[step] if step else v0_hbm

    def x_copies(step, y):
        return [
            remote(
                step,
                2 * y + side,
                source(step).at[0 if side else cx - 1, y],
                halo_x.at[step, side, y],
                towards(name_x, size_x, me_x, side),
            )
            for side in range(2)
        ]

    def y_copy(step, side, x, length):
        return remote(
            step,
            2 * cy + 3 * side + (0 if x == 0 else 1 if x == 1 else 2),
            source(step).at[pl.ds(x, length), 0 if side else cy - 1],
            halo_y.at[step, side, pl.ds(1 + x, length)],
            towards(name_y, size_y, me_y, side),
        )

    def y_middles(step):
        return [y_copy(step, side, 1, cx - 2) for side in range(2)]

    def y_ends(step, side):
        return [y_copy(step, side, x, 1) for x in (0, cx - 1)]

    def corner_copies(step, side):
        return [
            remote(
                step,
                2 * cy + 6 + 2 * side + end,
                halo_x.at[step, end, 0 if side else cy - 1],
                halo_y.at[step, side, end * (cx + 1)],
                towards(name_y, size_y, me_y, side),
            )
            for end in range(2)
        ]

    def start(copies):
        for copy in copies:
            copy.start()

    def arrive(copies):
        for copy in copies:
            copy.wait_recv()

    def row_sums(first, length):
        return lax.dot_general(
            jnp.ones((8, block), F32),
            sums[first : first + length],
            (((1,), (1,)), ((), ())),
            precision=lax.Precision.HIGHEST,
            preferred_element_type=F32,
        )[0:1]

    def put(field, position, value):
        high = value.astype(BF16)
        field[position, :width] = high
        field[position, width:] = (value - high.astype(F32)).astype(BF16)

    def put_turned(field, position, value, at_x, at_y):
        entry = at_x * 3 + at_y
        cosine, sine = turns[0, entry : entry + 1], turns[1, entry : entry + 1]
        real, imag = value[:half], value[half:]
        put(
            field,
            position,
            jnp.concatenate(
                [cosine * real - sine * imag, sine * real + cosine * imag], axis=0
            ),
        )

    def put_x(step, y):
        for side in range(2):
            put_turned(
                fields[step % 2],
                side * (cx + 1) * pitch + y + 1,
                halo_x[step, side, y],
                2 * side,
                1,
            )

    def put_y(step, side, x, at_x):
        put_turned(
            fields[step % 2],
            x * pitch + side * (cy + 1),
            halo_y[step, side, x],
            at_x,
            2 * side,
        )

    def prepare(x, y):
        i = x * cy + y
        count = counts[x, y]
        closing = isinstance(y, int) and (x, y) in final
        late_slot, late_place = jnp.int32(0), jnp.int32(nothing)
        from_x = lax.rem(me_x * cx + total_x - 1, total_x)
        from_y = lax.rem(me_y * cy + total_y - 1, total_y)
        for s in range(slots):
            partner = partners[x, y, s]
            partner_x = (partner * (((1 << 20) + total_y - 1) // total_y)) >> 20
            at_x = partner_x - from_x
            at_x = jnp.where(at_x < 0, at_x + total_x, at_x)
            at_y = partner - partner_x * total_y - from_y
            at_y = jnp.where(at_y < 0, at_y + total_y, at_y)
            at = jnp.where(s < count, at_x * pitch + at_y, nothing)
            table[i * slots + s] = at
            if closing:
                k = final.index((x, y))
                late_at = (0 if x == 0 else cx + 1) * pitch + final_y + 1
                is_late = at == late_at
                sooner[k * slots + s] = jnp.where(is_late, nothing, at)
                late_slot = jnp.where(is_late, s, late_slot)
                late_place = jnp.where(is_late, late_at, late_place)
            entry = landed[i, s]
            high = entry.astype(BF16)
            upper[i, s] = high
            lower[i, s] = (
                entry - high.astype(F32)
            ).astype(BF16)
        if closing:
            k = final.index((x, y))
            late[2 * k], late[2 * k + 1] = late_slot, late_place

    def split_dot(lhs, rhs):
        product = jnp.dot(lhs, rhs, preferred_element_type=F32)
        return product[:width, :block] + (
            product[width:, :block] + product[:width, block:] + product[width:, block:]
        )

    def gathered(step, x, y, entries, first):
        i = x * cy + y
        field = fields[step % 2]
        lhs = jnp.concatenate(
            [
                field[jnp.minimum(jnp.maximum(entries[first + s], 0), nothing)]
                for s in range(slots)
            ],
            axis=1,
        )
        high = upper[i].reshape(slots * block, block)
        low = lower[i].reshape(slots * block, block)
        value = split_dot(lhs, jnp.concatenate([high, low], axis=1))
        return 2.0 * value - vectors[step - 1][x, y] if step else value

    def meet(x, y, value):
        start_vector = v0[x, y]
        first_re, first_im = start_vector[:half], start_vector[half:]
        other_re, other_im = value[:half], value[half:]
        return (
            first_re * other_re + first_im * other_im,
            first_re * other_im - first_im * other_re,
        )

    def add_up(step, found):
        low = step * width
        sums[low : low + half] += sum(real for real, _ in found)
        sums[low + half : low + width] += sum(imag for _, imag in found)

    def advance(step, x, y):
        value = gathered(step, x, y, table, (x * cy + y) * slots)
        vectors[step + 1][x, y] = value
        if step + 1 < STEPS:
            put(fields[(step + 1) % 2], (x + 1) * pitch + y + 1, value)
        return meet(x, y, value)

    def sooner_part():
        for k, (x, y) in enumerate(final):
            last[x, y] = gathered(STEPS - 1, x, y, sooner, k * slots)

    def late_part():
        found = []
        field = fields[(STEPS - 1) % 2]
        for k, (x, y) in enumerate(final):
            i = x * cy + y
            slot = jnp.minimum(jnp.maximum(late[2 * k], 0), slots - 1)
            place = jnp.minimum(jnp.maximum(late[2 * k + 1], 0), nothing)
            rhs = jnp.concatenate([upper[i, slot], lower[i, slot]], axis=1)
            value = last[x, y] + 2.0 * split_dot(field[place], rhs)
            last[x, y] = value
            found.append(meet(x, y, value))
        add_up(STEPS - 1, found)

    def run(step, place, first, count, unroll):
        def body(k):
            cells = [place(first + k * unroll + u) for u in range(unroll)]
            if step == 0:
                for x, y in cells:
                    landing(x, y).wait()
            found = []
            for x, y in cells:
                if step == 0:
                    prepare(x, y)
                found.append(advance(step, x, y))
            add_up(step, found)

        if count == unroll:
            body(0)
        else:
            pl.loop(0, count // unroll)(body)

    for y in wire:
        start(x_copies(0, y))
    start(y_middles(0) + y_ends(0, 0) + y_ends(0, 1))
    sums[...] = jnp.zeros_like(sums)
    for field in fields:
        field[nothing] = jnp.zeros_like(field[nothing])
    row = lax.broadcasted_iota(jnp.int32, (16, block), 0)
    for copy in small:
        copy.wait()

    def crossing(at, me, size):
        low = (at == 0) & (me == 0)
        high = (at == 2) & (me == size - 1)
        return jnp.where(low, -1.0, jnp.where(high, 1.0, 0.0)).astype(F32)

    angle = kpoint[0] * crossing(row // 3, me_x, size_x)
    angle = angle + kpoint[1] * crossing(row % 3, me_y, size_y)
    turns[0], turns[1] = jnp.cos(angle), jnp.sin(angle)
    load_v0.wait()

    @pl.loop(0, cx * cy)
    def _(k):
        x, y = k // cy, k % cy
        put(field_a, (x + 1) * pitch + y + 1, v0[x, y])

    for step in range(STEPS):
        more = step + 1 < STEPS
        order = [mirror(step, y) for y in wire]
        near = 1 if step % 2 else 0
        run(step, interior, 0, early, 4)
        arrive(x_copies(step, order[0]))
        start(corner_copies(step, 1 - near))
        run(step, interior, early, inner - early, 4)
        arrive(x_copies(step, order[1]))
        start(corner_copies(step, near))
        put_x(step, order[0])
        put_x(step, order[1])
        arrive(y_middles(step) + y_ends(step, 0) + y_ends(step, 1))
        for side in range(2):

            @pl.loop(0, cx)
            def _(x):
                put_y(step, side, x + 1, 1)

        run(step, rim_y, 0, 2 * (cx - 2), 4)
        if more:
            start(y_middles(step + 1))
        for group, ys in enumerate(ready):
            closing = not more and group + 1 == len(ready)
            if closing:
                sooner_part()
                gather[..., : step * width] = row_sums(0, step * width)
            arrive(x_copies(step, order[group + 2]))
            put_x(step, order[group + 2])
            if group < 2:
                side = 1 - near if group == 0 else near
                arrive(corner_copies(step, side))
                for end in range(2):
                    put_y(step, side, end * (cx + 1), 2 * end)
            if closing:
                late_part()
            else:
                run(step, rim_x(step, ys), 0, 2 * len(ys), 2 * len(ys))
            if more:
                if len(ys) > 1:
                    ys = ys[::-1]
                for y in ys:
                    start(x_copies(step + 1, mirror(step, y)))
                if group < 2:
                    start(y_ends(step + 1, 1 if mirror(step, ys[0]) == 0 else 0))

    low = (STEPS - 1) * width
    gather[..., low:] = row_sums(low, width)
    if direct:
        stages = (("both", size_x * size_y),)
    else:
        stages = ((name_x, size_x), (name_y, size_y))
    found = gather[...]
    first = 0
    for name, size in stages:
        if name == "both":
            me = me_x * size_y + me_y
        else:
            me = me_x if name == name_x else me_y
        ring[first + me] = found
        copies = []
        for j in range(size - 1, 0, -1):
            if name == "both":
                peer = {
                    name_x: lax.rem(me_x + j // size_y, size_x),
                    name_y: lax.rem(me_y + j % size_y, size_y),
                }
            else:
                peer = {name: lax.rem(me + j, size)}
            copies.append(
                pltpu.make_async_remote_copy(
                    src_ref=ring.at[first + me],
                    dst_ref=ring.at[first + me],
                    send_sem=sum_send.at[first + j],
                    recv_sem=sum_recv.at[first + j],
                    device_id=peer,
                    device_id_type=MESH,
                )
            )
        start(copies)
        for copy in copies:
            copy.wait()
        found = ring[first]
        for j in range(1, size):
            found = found + ring[first + j]
        first += size
    scale = 1.0 / math.sqrt(total_x * total_y * block)
    for part in range(2 * STEPS):
        total[part // 2, part % 2 : part % 2 + 1] = (
            found[:, part * half : (part + 1) * half] * scale
        )
    for step in range(STEPS):
        for y in wire:
            for copy in x_copies(step, y):
                copy.wait_send()
        for side in range(2):
            for copy in y_ends(step, side) + corner_copies(step, side):
                copy.wait_send()
        for copy in y_middles(step):
            copy.wait_send()


def finish(last, total, last_out, total_out, sem):
    cx = last.shape[0]
    copies = [
        pltpu.make_async_copy(last.at[x], last_out.at[x], sem.at[x]) for x in range(cx)
    ]
    copies.append(pltpu.make_async_copy(total, total_out, sem.at[cx]))
    for copy in copies:
        copy.start()
    for copy in copies:
        copy.wait()


def shards(axes, probes, pair_blocks, partners, shifts, counts, kpoint):
    (name_x, size_x), (name_y, size_y) = axes
    cx, cy, width, block = probes.shape
    slots = pair_blocks.shape[2]
    cells = cx * cy
    rows = STEPS * width
    halo = (width, block)
    hbm = pl.BlockSpec(memory_space=pltpu.HBM)
    vmem = pl.BlockSpec(memory_space=pltpu.VMEM)
    dma = pltpu.SemaphoreType.DMA
    kinds = 2 * cy + 10
    direct = size_x // 2 < STEPS
    peers = size_x * size_y if direct else size_x + size_y
    last, found = pl.pallas_call(
        functools.partial(kernel, axes, direct),
        out_shape=(
            pltpu.VMEM(probes.shape, F32),
            pltpu.VMEM((STEPS, 2, width // 2), F32),
        ),
        in_specs=[hbm] * 5,
        out_specs=(vmem, vmem),
        scratch_shapes=[
            pltpu.SMEM(partners.shape, jnp.int32),
            pltpu.SMEM(counts.shape, jnp.int32),
            pltpu.SMEM(kpoint.shape, F32),
            pltpu.VMEM(probes.shape, F32),
            pltpu.VMEM(probes.shape, F32),
            pltpu.VMEM(probes.shape, F32),
            pltpu.VMEM((STEPS, 2, cy) + halo, F32),
            pltpu.VMEM((STEPS, 2, cx + 2) + halo, F32),
            pltpu.VMEM(((cx + 2) * (cy + 2) + 1, 2 * width, block), BF16),
            pltpu.VMEM(((cx + 2) * (cy + 2) + 1, 2 * width, block), BF16),
            pltpu.VMEM((cells, slots, block, block), F32),
            pltpu.VMEM((cells, slots, block, block), BF16),
            pltpu.VMEM((cells, slots, block, block), BF16),
            pltpu.VMEM((rows, block), F32),
            pltpu.VMEM((1, rows), F32),
            pltpu.VMEM((peers, 1, rows), F32),
            pltpu.SMEM((cells * slots,), jnp.int32),
            pltpu.SMEM((2 * cy * slots,), jnp.int32),
            pltpu.SMEM((4 * cy,), jnp.int32),
            pltpu.VMEM((2, 16, block), F32),
            dma(()),
            dma((3,)),
            dma((cells,)),
            dma((STEPS, kinds)),
            dma((STEPS, kinds)),
            dma((peers,)),
            dma((peers,)),
        ],
        compiler_params=pltpu.CompilerParams(
            collective_id=0, has_side_effects=True, vmem_limit_bytes=60_000_000
        ),
    )(partners, counts, kpoint, probes, pair_blocks)
    return pl.pallas_call(
        finish,
        out_shape=(
            jax.ShapeDtypeStruct(probes.shape, F32),
            jax.ShapeDtypeStruct((STEPS, 2, width // 2), F32),
        ),
        in_specs=[vmem, vmem],
        out_specs=(hbm, hbm),
        scratch_shapes=[dma((cx + 1,))],
    )(*(pltpu.with_memory_space_constraint(part, pltpu.VMEM) for part in (last, found)))


def solution(mesh):
    placed = (
        P("gx", "gy", None, None),
        P("gx", "gy", None, None, None),
        P("gx", "gy", None),
        P(None, "gx", "gy", None),
        P("gx", "gy"),
        P(),
    )
    axes = tuple((name, mesh.shape[name]) for name in ("gx", "gy"))
    return jax.shard_map(
        functools.partial(shards, axes),
        mesh=mesh,
        in_specs=placed,
        out_specs=(P("gx", "gy", None, None), P()),
        check_vma=False,
    )
```

```python
import functools
import math

import jax
import jax.numpy as jnp
from jax import lax
from jax.experimental import pallas as pl
from jax.experimental.pallas import tpu as pltpu
from jax.sharding import PartitionSpec as P

STEPS = 3
MESH = pl.DeviceIdType.MESH
F32, BF16 = jnp.float32, jnp.bfloat16


def kernel(
    axes, direct, partners_hbm, counts_hbm, kpoint_hbm, v0_hbm, blocks_hbm, last, total,
    partners, counts, kpoint, v0, v1, v2, halo_x, halo_y, field_a, field_b, landed, upper, lower, sums, gather, ring, table, sooner, late, turns,
    v0_sem, small_sem, land_sem, send_sem, recv_sem, sum_send, sum_recv,
):
    (name_x, size_x), (name_y, size_y) = axes
    cx, cy, width, block = v0.shape
    slots = landed.shape[1]
    half = width // 2
    pitch = cy + 2
    nothing = (cx + 2) * pitch
    me_x, me_y = lax.axis_index(name_x), lax.axis_index(name_y)
    total_x, total_y = cx * size_x, cy * size_y
    vectors = (v0, v1, v2, last)
    fields = (field_a, field_b)

    def landing(x, y):
        i = x * cy + y
        return pltpu.make_async_copy(blocks_hbm.at[x, y], landed.at[i], land_sem.at[i])

    inner = (cx - 2) * (cy - 2)

    def interior(k):
        return 1 + k // (cy - 2), 1 + k % (cy - 2)

    def rim_y(k):
        return 1 + k // 2, (k % 2) * (cy - 1)

    def mirror(step, y):
        return cy - 1 - y if step % 2 else y

    def rim_x(step, ys):
        return lambda k: ((k % 2) * (cx - 1), mirror(step, ys[k // 2]))

    wire = (0, cy - 1, cy - 2) + tuple(range(1, cy - 2))
    ready = ((cy - 1,), (0,)) + tuple((p - 1,) for p in range(2, cy - 3))
    ready = ready + ((cy - 4, cy - 3, cy - 2),)
    final = [rim_x(STEPS - 1, ready[-1])(k) for k in range(2 * len(ready[-1]))]
    final_y = mirror(STEPS - 1, wire[-1])
    early = inner // 2

    for signal_name, size, me in ((name_x, size_x, me_x), (name_y, size_y, me_y)):
        for j in range(1, size):
            pl.semaphore_signal(
                pltpu.get_barrier_semaphore(),
                inc=1,
                device_id={signal_name: lax.rem(me + j, size)},
                device_id_type=MESH,
            )
    load_v0 = pltpu.make_async_copy(v0_hbm, v0, v0_sem)
    load_v0.start()
    small = [
        pltpu.make_async_copy(there, here, small_sem.at[i])
        for i, (there, here) in enumerate(
            ((partners_hbm, partners), (counts_hbm, counts), (kpoint_hbm, kpoint))
        )
    ]
    for copy in small:
        copy.start()
    for place, count in (
        (interior, inner),
        (rim_y, 2 * (cx - 2)),
        *((rim_x(0, ys), 2 * len(ys)) for ys in ready),
    ):
        if count > 6:

            @pl.loop(0, count)
            def _(k):
                landing(*place(k)).start()
        else:
            for k in range(count):
                landing(*place(k)).start()
    pl.semaphore_wait(pltpu.get_barrier_semaphore(), size_x + size_y - 2)

    def towards(name, size, me, side):
        return {name: lax.rem(me + (size - 1 if side else 1), size)}

    def remote(step, kind, src, dst, peer):
        return pltpu.make_async_remote_copy(
            src_ref=src,
            dst_ref=dst,
            send_sem=send_sem.at[step, kind],
            recv_sem=recv_sem.at[step, kind],
            device_id=peer,
            device_id_type=MESH,
        )

    def source(step):
        return vectors[step] if step else v0_hbm

    def x_copies(step, y):
        return [
            remote(
                step,
                2 * y + side,
                source(step).at[0 if side else cx - 1, y],
                halo_x.at[step, side, y],
                towards(name_x, size_x, me_x, side),
            )
            for side in range(2)
        ]

    def start_x(step, y):
        for side in (1 - lax.rem(me_x, 2), lax.rem(me_x, 2)):
            remote(
                step,
                2 * y + side,
                source(step).at[(1 - side) * (cx - 1), y],
                halo_x.at[step, side, y],
                {name_x: lax.rem(me_x + 1 + side * (size_x - 2), size_x)},
            ).start()

    def y_copy(step, side, x, length):
        return remote(
            step,
            2 * cy + 3 * side + (0 if x == 0 else 1 if x == 1 else 2),
            source(step).at[pl.ds(x, length), 0 if side else cy - 1],
            halo_y.at[step, side, pl.ds(1 + x, length)],
            towards(name_y, size_y, me_y, side),
        )

    def y_middles(step):
        return [y_copy(step, side, 1, cx - 2) for side in range(2)]

    def y_ends(step, side):
        return [y_copy(step, side, x, 1) for x in (0, cx - 1)]

    def corner_copies(step, side):
        return [
            remote(
                step,
                2 * cy + 6 + 2 * side + end,
                halo_x.at[step, end, 0 if side else cy - 1],
                halo_y.at[step, side, end * (cx + 1)],
                towards(name_y, size_y, me_y, side),
            )
            for end in range(2)
        ]

    def start(copies):
        for copy in copies:
            copy.start()

    def arrive(copies):
        for copy in copies:
            copy.wait_recv()

    def row_sums(first, length):
        value = sums[first : first + length]
        parts = []
        for _ in range(3):
            part = value.astype(BF16)
            parts.append(part)
            value = value - part.astype(F32)
        whole = jnp.dot(
            jnp.concatenate(parts, axis=1),
            jnp.ones((3 * block, block), BF16),
            preferred_element_type=F32,
        )
        line = lax.broadcasted_iota(jnp.int32, (length, block), 0)
        lane = lax.broadcasted_iota(jnp.int32, (length, block), 1)
        row = jnp.sum(jnp.where(line == lane, whole, 0.0), axis=0, keepdims=True)
        return row[:, :length]

    def parts(value):
        high = value.astype(BF16)
        return high, (value - high.astype(F32)).astype(BF16)

    def put(field, position, value):
        field[position, :width], field[position, width:] = parts(value)

    def turned(value, at_x, at_y):
        entry = at_x * 3 + at_y
        cosine, sine = turns[0, entry : entry + 1], turns[1, entry : entry + 1]
        real, imag = value[:half], value[half:]
        return jnp.concatenate(
            [cosine * real - sine * imag, sine * real + cosine * imag], axis=0
        )

    def put_turned(field, position, value, at_x, at_y):
        put(field, position, turned(value, at_x, at_y))

    def put_x(step, y):
        for side in range(2):
            put_turned(
                fields[step % 2],
                side * (cx + 1) * pitch + y + 1,
                halo_x[step, side, y],
                2 * side,
                1,
            )

    def put_y(step, side, x, at_x):
        put_turned(
            fields[step % 2],
            x * pitch + side * (cy + 1),
            halo_y[step, side, x],
            at_x,
            2 * side,
        )

    def prepare(x, y):
        i = x * cy + y
        count = counts[x, y]
        closing = isinstance(y, int) and (x, y) in final
        late_slot, late_place = jnp.int32(0), jnp.int32(nothing)
        from_x = lax.rem(me_x * cx + total_x - 1, total_x)
        from_y = lax.rem(me_y * cy + total_y - 1, total_y)
        for s in range(slots):
            partner = partners[x, y, s]
            partner_x = (partner * (((1 << 20) + total_y - 1) // total_y)) >> 20
            at_x = partner_x - from_x
            at_x = jnp.where(at_x < 0, at_x + total_x, at_x)
            at_y = partner - partner_x * total_y - from_y
            at_y = jnp.where(at_y < 0, at_y + total_y, at_y)
            at = jnp.where(s < count, at_x * pitch + at_y, nothing)
            table[i * slots + s] = at
            if closing:
                k = final.index((x, y))
                late_at = (0 if x == 0 else cx + 1) * pitch + final_y + 1
                is_late = at == late_at
                sooner[k * slots + s] = jnp.where(is_late, nothing, at)
                late_slot = jnp.where(is_late, s, late_slot)
                late_place = jnp.where(is_late, late_at, late_place)
            entry = landed[i, s]
            high = entry.astype(BF16)
            upper[i, s] = high
            lower[i, s] = (
                entry - high.astype(F32)
            ).astype(BF16)
        if closing:
            k = final.index((x, y))
            late[2 * k], late[2 * k + 1] = late_slot, late_place

    def split_dot(lhs, rhs):
        product = jnp.dot(lhs, rhs, preferred_element_type=F32)
        return product[:width, :block] + (
            product[width:, :block] + product[:width, block:] + product[width:, block:]
        )

    def gathered(step, x, y, entries, first):
        i = x * cy + y
        field = fields[step % 2]
        lhs = jnp.concatenate(
            [
                field[jnp.minimum(jnp.maximum(entries[first + s], 0), nothing)]
                for s in range(slots)
            ],
            axis=1,
        )
        high = upper[i].reshape(slots * block, block)
        low = lower[i].reshape(slots * block, block)
        value = split_dot(lhs, jnp.concatenate([high, low], axis=1))
        return 2.0 * value - vectors[step - 1][x, y] if step else value

    def meet(x, y, value):
        start_vector = v0[x, y]
        first_re, first_im = start_vector[:half], start_vector[half:]
        other_re, other_im = value[:half], value[half:]
        return (
            first_re * other_re + first_im * other_im,
            first_re * other_im - first_im * other_re,
        )

    def add_up(step, found):
        low = step * width
        sums[low : low + half] += sum(real for real, _ in found)
        sums[low + half : low + width] += sum(imag for _, imag in found)

    def advance(step, x, y):
        value = gathered(step, x, y, table, (x * cy + y) * slots)
        vectors[step + 1][x, y] = value
        if step + 1 < STEPS:
            put(fields[(step + 1) % 2], (x + 1) * pitch + y + 1, value)
        return meet(x, y, value)

    def sooner_part():
        for k, (x, y) in enumerate(final):
            last[x, y] = gathered(STEPS - 1, x, y, sooner, k * slots)

    def late_part():
        halves = [
            parts(turned(halo_x[STEPS - 1, side, final_y], 2 * side, 1))
            for side in range(2)
        ]
        found = []
        for k, (x, y) in enumerate(final):
            i = x * cy + y
            slot = jnp.minimum(jnp.maximum(late[2 * k], 0), slots - 1)
            rhs = jnp.concatenate([upper[i, slot], lower[i, slot]], axis=1)
            lhs = jnp.concatenate(halves[1 if x else 0], axis=0)
            twice = jnp.where(late[2 * k + 1] < nothing, 2.0, 0.0).astype(F32)
            value = last[x, y] + twice * split_dot(lhs, rhs)
            last[x, y] = value
            found.append(meet(x, y, value))
        add_up(STEPS - 1, found)

    def run(step, place, first, count, unroll):
        def body(k):
            cells = [place(first + k * unroll + u) for u in range(unroll)]
            if step == 0:
                for x, y in cells:
                    landing(x, y).wait()
            found = []
            for x, y in cells:
                if step == 0:
                    prepare(x, y)
                found.append(advance(step, x, y))
            add_up(step, found)

        if count == unroll:
            body(0)
        else:
            pl.loop(0, count // unroll)(body)

    for y in wire:
        start_x(0, y)
    start(y_middles(0) + y_ends(0, 0) + y_ends(0, 1))
    sums[...] = jnp.zeros_like(sums)
    for field in fields:
        field[nothing] = jnp.zeros_like(field[nothing])
    row = lax.broadcasted_iota(jnp.int32, (16, block), 0)
    for copy in small:
        copy.wait()

    def crossing(at, me, size):
        low = (at == 0) & (me == 0)
        high = (at == 2) & (me == size - 1)
        return jnp.where(low, -1.0, jnp.where(high, 1.0, 0.0)).astype(F32)

    angle = kpoint[0] * crossing(row // 3, me_x, size_x)
    angle = angle + kpoint[1] * crossing(row % 3, me_y, size_y)
    turns[0], turns[1] = jnp.cos(angle), jnp.sin(angle)
    load_v0.wait()

    @pl.loop(0, cx * cy)
    def _(k):
        x, y = k // cy, k % cy
        put(field_a, (x + 1) * pitch + y + 1, v0[x, y])

    for step in range(STEPS):
        more = step + 1 < STEPS
        order = [mirror(step, y) for y in wire]
        near = 1 if step % 2 else 0
        run(step, interior, 0, early, 4)
        arrive(x_copies(step, order[0]))
        start(corner_copies(step, 1 - near))
        run(step, interior, early, inner - early, 4)
        arrive(x_copies(step, order[1]))
        start(corner_copies(step, near))
        put_x(step, order[0])
        put_x(step, order[1])
        arrive(y_middles(step) + y_ends(step, 0) + y_ends(step, 1))
        for side in range(2):

            @pl.loop(0, cx)
            def _(x):
                put_y(step, side, x + 1, 1)

        run(step, rim_y, 0, 2 * (cx - 2), 4)
        if more:
            start(y_middles(step + 1))
        for group, ys in enumerate(ready):
            closing = not more and group + 1 == len(ready)
            if closing:
                sooner_part()
                for k in range(step):
                    gather[..., k * width : (k + 1) * width] = row_sums(k * width, width)
            arrive(x_copies(step, order[group + 2]))
            if not closing:
                put_x(step, order[group + 2])
            if group < 2:
                side = 1 - near if group == 0 else near
                arrive(corner_copies(step, side))
                for end in range(2):
                    put_y(step, side, end * (cx + 1), 2 * end)
            if closing:
                late_part()
            else:
                run(step, rim_x(step, ys), 0, 2 * len(ys), 2 * len(ys))
            if more:
                if len(ys) > 1:
                    ys = ys[::-1]
                for y in ys:
                    start_x(step + 1, mirror(step, y))
                if group < 2:
                    start(y_ends(step + 1, 1 if mirror(step, ys[0]) == 0 else 0))

    low = (STEPS - 1) * width
    gather[..., low:] = row_sums(low, width)
    if direct:
        stages = (("both", size_x * size_y),)
    else:
        stages = ((name_x, size_x), (name_y, size_y))
    found = gather[...]
    first = 0
    for name, size in stages:
        if name == "both":
            me = me_x * size_y + me_y
        else:
            me = me_x if name == name_x else me_y
        ring[first + me] = found
        copies = []
        for j in range(size - 1, 0, -1):
            if name == "both":
                peer = {
                    name_x: lax.rem(me_x + j // size_y, size_x),
                    name_y: lax.rem(me_y + j % size_y, size_y),
                }
            else:
                peer = {name: lax.rem(me + j, size)}
            copies.append(
                pltpu.make_async_remote_copy(
                    src_ref=ring.at[first + me],
                    dst_ref=ring.at[first + me],
                    send_sem=sum_send.at[first + j],
                    recv_sem=sum_recv.at[first + j],
                    device_id=peer,
                    device_id_type=MESH,
                )
            )
        start(copies)
        for copy in copies:
            copy.wait()
        found = ring[first]
        for j in range(1, size):
            found = found + ring[first + j]
        first += size
    scale = 1.0 / math.sqrt(total_x * total_y * block)
    for part in range(2 * STEPS):
        total[part // 2, part % 2 : part % 2 + 1] = (
            found[:, part * half : (part + 1) * half] * scale
        )
    for step in range(STEPS):
        for y in wire:
            for copy in x_copies(step, y):
                copy.wait_send()
        for side in range(2):
            for copy in y_ends(step, side) + corner_copies(step, side):
                copy.wait_send()
        for copy in y_middles(step):
            copy.wait_send()


def finish(last, total, last_out, total_out, sem):
    copies = [
        pltpu.make_async_copy(total, total_out, sem.at[0]),
        pltpu.make_async_copy(last, last_out, sem.at[1]),
    ]
    for copy in copies:
        copy.start()
    for copy in copies:
        copy.wait()


def shards(axes, probes, pair_blocks, partners, shifts, counts, kpoint):
    (name_x, size_x), (name_y, size_y) = axes
    cx, cy, width, block = probes.shape
    slots = pair_blocks.shape[2]
    cells = cx * cy
    rows = STEPS * width
    halo = (width, block)
    hbm = pl.BlockSpec(memory_space=pltpu.HBM)
    vmem = pl.BlockSpec(memory_space=pltpu.VMEM)
    dma = pltpu.SemaphoreType.DMA
    kinds = 2 * cy + 10
    direct = size_x // 2 < STEPS
    peers = size_x * size_y if direct else size_x + size_y
    last, found = pl.pallas_call(
        functools.partial(kernel, axes, direct),
        out_shape=(
            pltpu.VMEM(probes.shape, F32),
            pltpu.VMEM((STEPS, 2, width // 2), F32),
        ),
        in_specs=[hbm] * 5,
        out_specs=(vmem, vmem),
        scratch_shapes=[
            pltpu.SMEM(partners.shape, jnp.int32),
            pltpu.SMEM(counts.shape, jnp.int32),
            pltpu.SMEM(kpoint.shape, F32),
            pltpu.VMEM(probes.shape, F32),
            pltpu.VMEM(probes.shape, F32),
            pltpu.VMEM(probes.shape, F32),
            pltpu.VMEM((STEPS, 2, cy) + halo, F32),
            pltpu.VMEM((STEPS, 2, cx + 2) + halo, F32),
            pltpu.VMEM(((cx + 2) * (cy + 2) + 1, 2 * width, block), BF16),
            pltpu.VMEM(((cx + 2) * (cy + 2) + 1, 2 * width, block), BF16),
            pltpu.VMEM((cells, slots, block, block), F32),
            pltpu.VMEM((cells, slots, block, block), BF16),
            pltpu.VMEM((cells, slots, block, block), BF16),
            pltpu.VMEM((rows, block), F32),
            pltpu.VMEM((1, rows), F32),
            pltpu.VMEM((peers, 1, rows), F32),
            pltpu.SMEM((cells * slots,), jnp.int32),
            pltpu.SMEM((2 * cy * slots,), jnp.int32),
            pltpu.SMEM((4 * cy,), jnp.int32),
            pltpu.VMEM((2, 16, block), F32),
            dma(()),
            dma((3,)),
            dma((cells,)),
            dma((STEPS, kinds)),
            dma((STEPS, kinds)),
            dma((peers,)),
            dma((peers,)),
        ],
        compiler_params=pltpu.CompilerParams(
            collective_id=0, has_side_effects=True, vmem_limit_bytes=60_000_000
        ),
    )(partners, counts, kpoint, probes, pair_blocks)
    return pl.pallas_call(
        finish,
        out_shape=(
            jax.ShapeDtypeStruct(probes.shape, F32),
            jax.ShapeDtypeStruct((STEPS, 2, width // 2), F32),
        ),
        in_specs=[vmem, vmem],
        out_specs=(hbm, hbm),
        scratch_shapes=[dma((2,))],
    )(*(pltpu.with_memory_space_constraint(part, pltpu.VMEM) for part in (last, found)))


def solution(mesh):
    placed = (
        P("gx", "gy", None, None),
        P("gx", "gy", None, None, None),
        P("gx", "gy", None),
        P(None, "gx", "gy", None),
        P("gx", "gy"),
        P(),
    )
    axes = tuple((name, mesh.shape[name]) for name in ("gx", "gy"))
    return jax.shard_map(
        functools.partial(shards, axes),
        mesh=mesh,
        in_specs=placed,
        out_specs=(P("gx", "gy", None, None), P()),
        check_vma=False,
    )
```

```python
import functools
import math

import jax
import jax.numpy as jnp
from jax import lax
from jax.experimental import pallas as pl
from jax.experimental.pallas import tpu as pltpu
from jax.sharding import PartitionSpec as P

STEPS = 3
MESH = pl.DeviceIdType.MESH
F32, BF16 = jnp.float32, jnp.bfloat16


def kernel(
    axes, direct, partners_hbm, counts_hbm, kpoint_hbm, v0_hbm, blocks_hbm, last, total,
    partners, counts, kpoint, v0, v1, v2, halo_x, halo_y, field_a, field_b, landed, upper, lower, sums, gather, ring, table, sooner, late, turns,
    v0_sem, small_sem, land_sem, send_sem, recv_sem, sum_send, sum_recv,
):
    (name_x, size_x), (name_y, size_y) = axes
    cx, cy, width, block = v0.shape
    slots = landed.shape[1]
    half = width // 2
    pitch = cy + 2
    nothing = (cx + 2) * pitch
    me_x, me_y = lax.axis_index(name_x), lax.axis_index(name_y)
    total_x, total_y = cx * size_x, cy * size_y
    vectors = (v0, v1, v2, last)
    fields = (field_a, field_b)

    def landing(x, y):
        i = x * cy + y
        return pltpu.make_async_copy(blocks_hbm.at[x, y], landed.at[i], land_sem.at[i])

    inner = (cx - 2) * (cy - 2)

    def interior(k):
        return 1 + k // (cy - 2), 1 + k % (cy - 2)

    def rim_y(k):
        return 1 + k // 2, (k % 2) * (cy - 1)

    def mirror(step, y):
        return cy - 1 - y if step % 2 else y

    def rim_x(step, ys):
        return lambda k: ((k % 2) * (cx - 1), mirror(step, ys[k // 2]))

    wire = (0, cy - 1, cy - 2) + tuple(range(1, cy - 2))
    ready = ((cy - 1,), (0,)) + tuple((p - 1,) for p in range(2, cy - 3))
    ready = ready + ((cy - 4, cy - 3, cy - 2),)
    final = [rim_x(STEPS - 1, ready[-1])(k) for k in range(2 * len(ready[-1]))]
    final_y = mirror(STEPS - 1, wire[-1])
    early = inner // 2

    for signal_name, size, me in ((name_x, size_x, me_x), (name_y, size_y, me_y)):
        for j in range(1, size):
            pl.semaphore_signal(
                pltpu.get_barrier_semaphore(),
                inc=1,
                device_id={signal_name: lax.rem(me + j, size)},
                device_id_type=MESH,
            )
    load_v0 = pltpu.make_async_copy(v0_hbm, v0, v0_sem)
    load_v0.start()
    small = [
        pltpu.make_async_copy(there, here, small_sem.at[i])
        for i, (there, here) in enumerate(
            ((partners_hbm, partners), (counts_hbm, counts), (kpoint_hbm, kpoint))
        )
    ]
    for copy in small:
        copy.start()
    for place, count in (
        (interior, inner),
        (rim_y, 2 * (cx - 2)),
        *((rim_x(0, ys), 2 * len(ys)) for ys in ready),
    ):
        if count > 6:

            @pl.loop(0, count)
            def _(k):
                landing(*place(k)).start()
        else:
            for k in range(count):
                landing(*place(k)).start()
    pl.semaphore_wait(pltpu.get_barrier_semaphore(), size_x + size_y - 2)

    def towards(name, size, me, side):
        return {name: lax.rem(me + (size - 1 if side else 1), size)}

    def remote(step, kind, src, dst, peer):
        return pltpu.make_async_remote_copy(
            src_ref=src,
            dst_ref=dst,
            send_sem=send_sem.at[step, kind],
            recv_sem=recv_sem.at[step, kind],
            device_id=peer,
            device_id_type=MESH,
        )

    def source(step):
        return vectors[step] if step else v0_hbm

    def x_copies(step, y):
        return [
            remote(
                step,
                2 * y + side,
                source(step).at[0 if side else cx - 1, y],
                halo_x.at[step, side, y],
                towards(name_x, size_x, me_x, side),
            )
            for side in range(2)
        ]

    def start_x(step, y):
        for side in (1 - lax.rem(me_x, 2), lax.rem(me_x, 2)):
            remote(
                step,
                2 * y + side,
                source(step).at[(1 - side) * (cx - 1), y],
                halo_x.at[step, side, y],
                {name_x: lax.rem(me_x + 1 + side * (size_x - 2), size_x)},
            ).start()

    def y_copy(step, side, x, length):
        return remote(
            step,
            2 * cy + 3 * side + (0 if x == 0 else 1 if x == 1 else 2),
            source(step).at[pl.ds(x, length), 0 if side else cy - 1],
            halo_y.at[step, side, pl.ds(1 + x, length)],
            towards(name_y, size_y, me_y, side),
        )

    def y_middles(step):
        return [y_copy(step, side, 1, cx - 2) for side in range(2)]

    def y_ends(step, side):
        return [y_copy(step, side, x, 1) for x in (0, cx - 1)]

    def corner_copies(step, side):
        return [
            remote(
                step,
                2 * cy + 6 + 2 * side + end,
                halo_x.at[step, end, 0 if side else cy - 1],
                halo_y.at[step, side, end * (cx + 1)],
                towards(name_y, size_y, me_y, side),
            )
            for end in range(2)
        ]

    def start(copies):
        for copy in copies:
            copy.start()

    def arrive(copies):
        for copy in copies:
            copy.wait_recv()

    def row_sums(first, length):
        value = sums[first : first + length]
        parts = []
        for _ in range(3):
            part = value.astype(BF16)
            parts.append(part)
            value = value - part.astype(F32)
        whole = jnp.dot(
            jnp.concatenate(parts, axis=1),
            jnp.ones((3 * block, block), BF16),
            preferred_element_type=F32,
        )
        line = lax.broadcasted_iota(jnp.int32, (length, block), 0)
        lane = lax.broadcasted_iota(jnp.int32, (length, block), 1)
        row = jnp.sum(jnp.where(line == lane, whole, 0.0), axis=0, keepdims=True)
        return row[:, :length]

    def parts(value):
        high = value.astype(BF16)
        return high, (value - high.astype(F32)).astype(BF16)

    def put(field, position, value):
        field[position, :width], field[position, width:] = parts(value)

    def turned(value, at_x, at_y):
        entry = at_x * 3 + at_y
        cosine, sine = turns[0, entry : entry + 1], turns[1, entry : entry + 1]
        real, imag = value[:half], value[half:]
        return jnp.concatenate(
            [cosine * real - sine * imag, sine * real + cosine * imag], axis=0
        )

    def put_turned(field, position, value, at_x, at_y):
        put(field, position, turned(value, at_x, at_y))

    def put_x(step, y):
        for side in range(2):
            put_turned(
                fields[step % 2],
                side * (cx + 1) * pitch + y + 1,
                halo_x[step, side, y],
                2 * side,
                1,
            )

    def put_y(step, side, x, at_x):
        put_turned(
            fields[step % 2],
            x * pitch + side * (cy + 1),
            halo_y[step, side, x],
            at_x,
            2 * side,
        )

    def prepare(x, y):
        i = x * cy + y
        count = counts[x, y]
        closing = isinstance(y, int) and (x, y) in final
        late_slot, late_place = jnp.int32(0), jnp.int32(nothing)
        from_x = lax.rem(me_x * cx + total_x - 1, total_x)
        from_y = lax.rem(me_y * cy + total_y - 1, total_y)
        for s in range(slots):
            partner = partners[x, y, s]
            partner_x = (partner * (((1 << 20) + total_y - 1) // total_y)) >> 20
            at_x = partner_x - from_x
            at_x = jnp.where(at_x < 0, at_x + total_x, at_x)
            at_y = partner - partner_x * total_y - from_y
            at_y = jnp.where(at_y < 0, at_y + total_y, at_y)
            at = jnp.where(s < count, at_x * pitch + at_y, nothing)
            table[i * slots + s] = at
            if closing:
                k = final.index((x, y))
                late_at = (0 if x == 0 else cx + 1) * pitch + final_y + 1
                is_late = at == late_at
                sooner[k * slots + s] = jnp.where(is_late, nothing, at)
                late_slot = jnp.where(is_late, s, late_slot)
                late_place = jnp.where(is_late, late_at, late_place)
            entry = landed[i, s]
            high = entry.astype(BF16)
            upper[i, s] = high
            lower[i, s] = (
                entry - high.astype(F32)
            ).astype(BF16)
        if closing:
            k = final.index((x, y))
            late[2 * k], late[2 * k + 1] = late_slot, late_place

    def split_dot(lhs, rhs):
        product = jnp.dot(lhs, rhs, preferred_element_type=F32)
        return product[:width, :block] + (
            product[width:, :block] + product[:width, block:] + product[width:, block:]
        )

    def gathered(step, x, y, entries, first):
        i = x * cy + y
        field = fields[step % 2]
        lhs = jnp.concatenate(
            [
                field[jnp.minimum(jnp.maximum(entries[first + s], 0), nothing)]
                for s in range(slots)
            ],
            axis=1,
        )
        high = upper[i].reshape(slots * block, block)
        low = lower[i].reshape(slots * block, block)
        value = split_dot(lhs, jnp.concatenate([high, low], axis=1))
        return 2.0 * value - vectors[step - 1][x, y] if step else value

    def meet(x, y, value):
        start_vector = v0[x, y]
        first_re, first_im = start_vector[:half], start_vector[half:]
        other_re, other_im = value[:half], value[half:]
        return (
            first_re * other_re + first_im * other_im,
            first_re * other_im - first_im * other_re,
        )

    def add_up(step, found):
        low = step * width
        sums[low : low + half] += sum(real for real, _ in found)
        sums[low + half : low + width] += sum(imag for _, imag in found)

    def advance(step, x, y):
        value = gathered(step, x, y, table, (x * cy + y) * slots)
        vectors[step + 1][x, y] = value
        if step + 1 < STEPS:
            put(fields[(step + 1) % 2], (x + 1) * pitch + y + 1, value)
        return meet(x, y, value)

    def sooner_part():
        for k, (x, y) in enumerate(final):
            last[x, y] = gathered(STEPS - 1, x, y, sooner, k * slots)

    def late_part():
        halves = [
            parts(turned(halo_x[STEPS - 1, side, final_y], 2 * side, 1))
            for side in range(2)
        ]
        found = []
        for k, (x, y) in enumerate(final):
            i = x * cy + y
            slot = jnp.minimum(jnp.maximum(late[2 * k], 0), slots - 1)
            rhs = jnp.concatenate([upper[i, slot], lower[i, slot]], axis=1)
            lhs = jnp.concatenate(halves[1 if x else 0], axis=0)
            twice = jnp.where(late[2 * k + 1] < nothing, 2.0, 0.0).astype(F32)
            value = last[x, y] + twice * split_dot(lhs, rhs)
            last[x, y] = value
            found.append(meet(x, y, value))
        add_up(STEPS - 1, found)

    def run(step, place, first, count, unroll):
        def body(k):
            cells = [place(first + k * unroll + u) for u in range(unroll)]
            if step == 0:
                for x, y in cells:
                    landing(x, y).wait()
            found = []
            for x, y in cells:
                if step == 0:
                    prepare(x, y)
                found.append(advance(step, x, y))
            add_up(step, found)

        if count == unroll:
            body(0)
        else:
            pl.loop(0, count // unroll)(body)

    for y in wire:
        start_x(0, y)
    start(y_ends(0, 0) + y_ends(0, 1) + y_middles(0))
    sums[...] = jnp.zeros_like(sums)
    for field in fields:
        field[nothing] = jnp.zeros_like(field[nothing])
    row = lax.broadcasted_iota(jnp.int32, (16, block), 0)
    for copy in small:
        copy.wait()

    def crossing(at, me, size):
        low = (at == 0) & (me == 0)
        high = (at == 2) & (me == size - 1)
        return jnp.where(low, -1.0, jnp.where(high, 1.0, 0.0)).astype(F32)

    angle = kpoint[0] * crossing(row // 3, me_x, size_x)
    angle = angle + kpoint[1] * crossing(row % 3, me_y, size_y)
    turns[0], turns[1] = jnp.cos(angle), jnp.sin(angle)
    load_v0.wait()

    @pl.loop(0, cx * cy)
    def _(k):
        x, y = k // cy, k % cy
        put(field_a, (x + 1) * pitch + y + 1, v0[x, y])

    for step in range(STEPS):
        more = step + 1 < STEPS
        order = [mirror(step, y) for y in wire]
        near = 1 if step % 2 else 0
        run(step, interior, 0, early, 4)
        arrive(x_copies(step, order[0]))
        start(corner_copies(step, 1 - near))
        run(step, interior, early, inner - early, 4)
        arrive(x_copies(step, order[1]))
        start(corner_copies(step, near))
        put_x(step, order[0])
        put_x(step, order[1])
        arrive(y_middles(step) + y_ends(step, 0) + y_ends(step, 1))
        for side in range(2):

            @pl.loop(0, cx)
            def _(x):
                put_y(step, side, x + 1, 1)

        run(step, rim_y, 0, 2 * (cx - 2), 4)
        if more:
            start(y_middles(step + 1))
        for group, ys in enumerate(ready):
            closing = not more and group + 1 == len(ready)
            if closing:
                sooner_part()
                for k in range(step):
                    gather[..., k * width : (k + 1) * width] = row_sums(k * width, width)
            arrive(x_copies(step, order[group + 2]))
            if not closing:
                put_x(step, order[group + 2])
            if group < 2:
                side = 1 - near if group == 0 else near
                arrive(corner_copies(step, side))
                for end in range(2):
                    put_y(step, side, end * (cx + 1), 2 * end)
            if closing:
                late_part()
            else:
                run(step, rim_x(step, ys), 0, 2 * len(ys), 2 * len(ys))
            if more:
                if len(ys) > 1:
                    ys = ys[::-1]
                for y in ys:
                    start_x(step + 1, mirror(step, y))
                if group < 2:
                    start(y_ends(step + 1, 1 if mirror(step, ys[0]) == 0 else 0))

    low = (STEPS - 1) * width
    gather[..., low:] = row_sums(low, width)
    if direct:
        stages = (("both", size_x * size_y),)
    else:
        stages = ((name_x, size_x), (name_y, size_y))
    found = gather[...]
    first = 0
    for name, size in stages:
        if name == "both":
            me = me_x * size_y + me_y
        else:
            me = me_x if name == name_x else me_y
        ring[first + me] = found
        copies = []
        for j in range(size - 1, 0, -1):
            if name == "both":
                step_x = (j // size_y) * (1 + lax.rem(me_x, 2) * (size_x - 2))
                step_x = lax.rem(step_x, size_x)
                peer = {
                    name_x: lax.rem(me_x + step_x, size_x),
                    name_y: lax.rem(me_y + j % size_y, size_y),
                }
                offset = step_x * size_y + j % size_y
            else:
                peer = {name: lax.rem(me + j, size)}
                offset = j
            copies.append(
                pltpu.make_async_remote_copy(
                    src_ref=ring.at[first + me],
                    dst_ref=ring.at[first + me],
                    send_sem=sum_send.at[first + offset],
                    recv_sem=sum_recv.at[first + offset],
                    device_id=peer,
                    device_id_type=MESH,
                )
            )
        start(copies)
        for copy in copies:
            copy.wait()
        found = ring[first]
        for j in range(1, size):
            found = found + ring[first + j]
        first += size
    scale = 1.0 / math.sqrt(total_x * total_y * block)
    for part in range(2 * STEPS):
        total[part // 2, part % 2 : part % 2 + 1] = (
            found[:, part * half : (part + 1) * half] * scale
        )
    for step in range(STEPS):
        for y in wire:
            for copy in x_copies(step, y):
                copy.wait_send()
        for side in range(2):
            for copy in y_ends(step, side) + corner_copies(step, side):
                copy.wait_send()
        for copy in y_middles(step):
            copy.wait_send()


def finish(last, total, last_out, total_out, sem):
    copies = [
        pltpu.make_async_copy(total, total_out, sem.at[0]),
        pltpu.make_async_copy(last, last_out, sem.at[1]),
    ]
    for copy in copies:
        copy.start()
    for copy in copies:
        copy.wait()


def shards(axes, probes, pair_blocks, partners, shifts, counts, kpoint):
    (name_x, size_x), (name_y, size_y) = axes
    cx, cy, width, block = probes.shape
    slots = pair_blocks.shape[2]
    cells = cx * cy
    rows = STEPS * width
    halo = (width, block)
    hbm = pl.BlockSpec(memory_space=pltpu.HBM)
    vmem = pl.BlockSpec(memory_space=pltpu.VMEM)
    dma = pltpu.SemaphoreType.DMA
    kinds = 2 * cy + 10
    direct = size_x // 2 < STEPS
    peers = size_x * size_y if direct else size_x + size_y
    last, found = pl.pallas_call(
        functools.partial(kernel, axes, direct),
        out_shape=(
            pltpu.VMEM(probes.shape, F32),
            pltpu.VMEM((STEPS, 2, width // 2), F32),
        ),
        in_specs=[hbm] * 5,
        out_specs=(vmem, vmem),
        scratch_shapes=[
            pltpu.SMEM(partners.shape, jnp.int32),
            pltpu.SMEM(counts.shape, jnp.int32),
            pltpu.SMEM(kpoint.shape, F32),
            pltpu.VMEM(probes.shape, F32),
            pltpu.VMEM(probes.shape, F32),
            pltpu.VMEM(probes.shape, F32),
            pltpu.VMEM((STEPS, 2, cy) + halo, F32),
            pltpu.VMEM((STEPS, 2, cx + 2) + halo, F32),
            pltpu.VMEM(((cx + 2) * (cy + 2) + 1, 2 * width, block), BF16),
            pltpu.VMEM(((cx + 2) * (cy + 2) + 1, 2 * width, block), BF16),
            pltpu.VMEM((cells, slots, block, block), F32),
            pltpu.VMEM((cells, slots, block, block), BF16),
            pltpu.VMEM((cells, slots, block, block), BF16),
            pltpu.VMEM((rows, block), F32),
            pltpu.VMEM((1, rows), F32),
            pltpu.VMEM((peers, 1, rows), F32),
            pltpu.SMEM((cells * slots,), jnp.int32),
            pltpu.SMEM((2 * cy * slots,), jnp.int32),
            pltpu.SMEM((4 * cy,), jnp.int32),
            pltpu.VMEM((2, 16, block), F32),
            dma(()),
            dma((3,)),
            dma((cells,)),
            dma((STEPS, kinds)),
            dma((STEPS, kinds)),
            dma((peers,)),
            dma((peers,)),
        ],
        compiler_params=pltpu.CompilerParams(
            collective_id=0, has_side_effects=True, vmem_limit_bytes=60_000_000
        ),
    )(partners, counts, kpoint, probes, pair_blocks)
    return pl.pallas_call(
        finish,
        out_shape=(
            jax.ShapeDtypeStruct(probes.shape, F32),
            jax.ShapeDtypeStruct((STEPS, 2, width // 2), F32),
        ),
        in_specs=[vmem, vmem],
        out_specs=(hbm, hbm),
        scratch_shapes=[dma((2,))],
    )(*(pltpu.with_memory_space_constraint(part, pltpu.VMEM) for part in (last, found)))


def solution(mesh):
    placed = (
        P("gx", "gy", None, None),
        P("gx", "gy", None, None, None),
        P("gx", "gy", None),
        P(None, "gx", "gy", None),
        P("gx", "gy"),
        P(),
    )
    axes = tuple((name, mesh.shape[name]) for name in ("gx", "gy"))
    return jax.shard_map(
        functools.partial(shards, axes),
        mesh=mesh,
        in_specs=placed,
        out_specs=(P("gx", "gy", None, None), P()),
        check_vma=False,
    )
```
